32 devices in a mesh: gx: 8 (over z, core), gy: 4 (over y, x).
Axes of the slice: x: 2, y: 2, z: 4, core: 2. Of those that a mesh axis runs over, the one named last changes fastest.
Arguments:
- tangent_e: float32 [3, 64, 64, 256], P(None, 'gx', 'gy'), may hold values from -6 to 6
- tangent_h: float32 [3, 64, 64, 256], P(None, 'gx', 'gy'), may hold values from -6 to 6
- forward_e: float32 [3, 64, 64, 4], P(None, 'gx', 'gy'), may hold values from -6 to 6
- forward_h: float32 [3, 64, 64, 4], P(None, 'gx', 'gy'), may hold values from -6 to 6
- class_map: int32 [64, 64, 4], P('gx', 'gy'), may hold values from 0 to 63
- material: int32 [64, 64, 4], P('gx', 'gy'), may hold values from 0 to 3
- permittivity: float32 [4], replicated, may hold values from 1 to 4
- contrast: float32 [4], replicated, may hold values from 0.5 to 2
- order_list: int32 [1024, 2], replicated, may hold values from -16 to 16
Outputs:
- new_tangent_e: float32 [3, 64, 64, 256], P(None, 'gx', 'gy')
- new_tangent_h: float32 [3, 64, 64, 256], P(None, 'gx', 'gy')
- order_sens: float32 [1024, 256], P(('gx', 'gy'))
The draws below stay inside these ranges and needn't reach their ends.
Inputs may be any that keep to these rules, and one draw needn't show every extreme that they name: `class_map`: feature class of each cell, naming its tangent direction.
All inputs are finite; a program needn't handle non-finite values.
Results may differ from the reference program's by a relative error of at most 0.0003.
Values sent between devices are 32-bit elements; how exact they have to be, the bound alone decides.
A program may use at most 64 MiB of HBM per device.

```python
import math
import jax
import jax.numpy as jnp
from jax import lax

NZ = 4
DIRS = 64
NMAT = 4
ORDERS = 1024
ORDER_MAX = 16
STEPS = 2
NX = 64
NY = 64


def with_ends(result, key, least, largest):
    extent = result.shape
    index_at = [jax.random.randint(jax.random.fold_in(key, axis), (), 0, extent[axis]) for axis in range(len(extent))]
    result = result.at[tuple(index_at)].set(least)
    longest = extent.index(max(extent))
    index_at[longest] = (index_at[longest] + 1) % extent[longest]
    return result.at[tuple(index_at)].set(largest)


def levels(key, extent, pieces, smallest, top_value):
    factor_of = 1.0
    for dim, shards_of in pieces:
        steps = jax.random.uniform(jax.random.fold_in(jax.random.fold_in(key, 6), dim), (shards_of,), jnp.float32, smallest / len(pieces), top_value / len(pieces))
        factor_of = factor_of * jnp.repeat(jnp.exp(steps), extent[dim] // shards_of).reshape((-1,) + (1,) * (len(extent) - 1 - dim))
    return factor_of


def centred(key, extent, deviation, most, cuts=(), kind=jnp.bfloat16):
    entries = deviation * jax.random.normal(key, extent, jnp.float32)
    if cuts:
        entries = entries * levels(key, extent, cuts, -0.22, 0.18)
    return jnp.clip(entries, -most, most).astype(kind)


def setup_inputs(seed: int = 0) -> dict:
    streams_of = jax.random.split(jax.random.key(seed), 10)
    return {
        "tangent_e": centred(streams_of[0], (3, NX, NY, NZ * DIRS), 1.0, 6.0, ((1, 8), (2, 4)), jnp.float32),
        "tangent_h": centred(streams_of[1], (3, NX, NY, NZ * DIRS), 1.0, 6.0, ((1, 8), (2, 4)), jnp.float32),
        "forward_e": centred(streams_of[2], (3, NX, NY, NZ), 1.0, 6.0, ((1, 8), (2, 4)), jnp.float32),
        "forward_h": centred(streams_of[3], (3, NX, NY, NZ), 1.0, 6.0, ((1, 8), (2, 4)), jnp.float32),
        "class_map": with_ends(jax.random.randint(streams_of[4], (NX, NY, NZ), 0, DIRS), jax.random.fold_in(streams_of[4], 1), 0, DIRS - 1).astype(jnp.int32),
        "material": with_ends(jax.random.randint(streams_of[5], (NX, NY, NZ), 0, NMAT), jax.random.fold_in(streams_of[5], 1), 0, NMAT - 1).astype(jnp.int32),
        "permittivity": jnp.clip(jnp.exp(jax.random.uniform(streams_of[6], (NMAT,), jnp.float32, math.log(1.0), math.log(4.0))), 1.0, 4.0),
        "contrast": jnp.clip(jnp.exp(jax.random.uniform(streams_of[7], (NMAT,), jnp.float32, math.log(0.5), math.log(2.0))), 0.5, 2.0),
        "order_list": with_ends(jax.random.randint(streams_of[8], (ORDERS, 2), -ORDER_MAX, ORDER_MAX + 1), jax.random.fold_in(streams_of[8], 1), -ORDER_MAX, ORDER_MAX).astype(jnp.int32),
    }


time_step = 0.5

def next_z(field, unit):
    return jnp.concatenate([field[..., unit:], jnp.zeros_like(field[..., :unit])], -1)

def prev_z(field, unit):
    return jnp.concatenate([jnp.zeros_like(field[..., :unit]), field[..., :-unit]], -1)

def curl_forward(field, unit):
    field_x, field_y, field_z = (field[0], field[1], field[2])
    curl_x = jnp.roll(field_z, -1, 1) - field_z - (next_z(field_y, unit) - field_y)
    curl_y = next_z(field_x, unit) - field_x - (jnp.roll(field_z, -1, 0) - field_z)
    curl_z = jnp.roll(field_y, -1, 0) - field_y - (jnp.roll(field_x, -1, 1) - field_x)
    return jnp.stack([curl_x, curl_y, curl_z])

def curl_backward(field, unit):
    field_x, field_y, field_z = (field[0], field[1], field[2])
    curl_x = field_z - jnp.roll(field_z, 1, 1) - (field_y - prev_z(field_y, unit))
    curl_y = field_x - prev_z(field_x, unit) - (field_z - jnp.roll(field_z, 1, 0))
    curl_z = field_y - jnp.roll(field_y, 1, 0) - (field_x - jnp.roll(field_x, 1, 1))
    return jnp.stack([curl_x, curl_y, curl_z])

def cell_values(material, table):
    hits = (material[..., None] == jnp.arange(table.shape[0], dtype=jnp.int32)).astype(jnp.float32)
    return lax.optimization_barrier(jnp.sum(hits * table, -1))

def reference(tangent_e, tangent_h, forward_e, forward_h, class_map, material, permittivity, contrast, order_list):
    eps_cell = cell_values(material, permittivity)
    inverse = time_step / eps_cell
    coef = time_step * cell_values(material, contrast) / (eps_cell * eps_cell)
    inverse_wide = jnp.repeat(inverse, DIRS, axis=-1)
    onehot = (class_map[..., None] == jnp.arange(DIRS, dtype=jnp.int32)).astype(jnp.float32)
    for step in range(STEPS):
        forward_h = forward_h - time_step * curl_forward(forward_e, 1)
        tangent_h = tangent_h - time_step * curl_forward(tangent_e, DIRS)
        curl_fwd = curl_backward(forward_h, 1)
        forward_e = forward_e + inverse[None] * curl_fwd
        curl_tan = curl_backward(tangent_h, DIRS)
        source = ((coef[None] * curl_fwd)[..., None] * onehot[None]).reshape(tangent_e.shape)
        tangent_e = tangent_e + inverse_wide[None] * curl_tan - source
    top = tangent_e[0:2, :, :, (NZ - 1) * DIRS:]
    top = jnp.transpose(top, (1, 2, 0, 3)).reshape(NX * NY, 2 * DIRS)
    xs = jnp.arange(NX, dtype=jnp.int32)
    ys = jnp.arange(NY, dtype=jnp.int32)
    factor = 2.0 * math.pi / (NX * NY)
    scale = 1.0 / math.sqrt(NX * NY)

    def block(pairs):
        order_m = pairs[:, 0]
        order_n = pairs[:, 1]
        count = pairs.shape[0]
        index = order_m[:, None, None] * xs[None, :, None] * NY + order_n[:, None, None] * ys[None, None, :] * NX
        index = jnp.mod(index, NX * NY).reshape(count, NX * NY)
        theta = index.astype(jnp.float32) * factor
        real = jnp.dot(jnp.cos(theta), top, precision=lax.Precision.HIGHEST, preferred_element_type=jnp.float32)
        imag = -jnp.dot(jnp.sin(theta), top, precision=lax.Precision.HIGHEST, preferred_element_type=jnp.float32)
        both = jnp.stack([real.reshape(count, 2, DIRS), imag.reshape(count, 2, DIRS)], 2)
        return both.reshape(count, 4 * DIRS) * scale
    order_sens = lax.map(block, order_list.reshape(ORDERS // 128, 128, 2)).reshape(ORDERS, 4 * DIRS)
    return (tangent_e, tangent_h, order_sens)
```

```python
import functools
import math

import jax
import jax.numpy as jnp
from jax import lax
from jax.experimental import pallas as pl
from jax.experimental.pallas import tpu as pltpu
from jax.sharding import PartitionSpec as P

DIRS = 64
STEPS = 2
LAYERS = 4
WIDE = LAYERS * DIRS
HALF = WIDE // 2
HIGHEST = lax.Precision.HIGHEST
time_step = 0.5


def lanes_of(shape):
    return lax.broadcasted_iota(jnp.int32, shape, len(shape) - 1)


def sublanes_of(shape):
    return lax.broadcasted_iota(jnp.int32, shape, len(shape) - 2)


def next_z(f):
    return jnp.where(lanes_of(f.shape) < WIDE - DIRS, pltpu.roll(f, WIDE - DIRS, f.ndim - 1), 0.0)


def prev_z(f):
    return jnp.where(lanes_of(f.shape) >= DIRS, pltpu.roll(f, DIRS, f.ndim - 1), 0.0)


def after_rows(f, row):
    n = f.shape[-2]
    return jnp.where(sublanes_of(f.shape) == n - 1, row, pltpu.roll(f, n - 1, f.ndim - 2))


def before_rows(f, row):
    return jnp.where(sublanes_of(f.shape) == 0, row, pltpu.roll(f, 1, f.ndim - 2))


def after_x(f, plane):
    return jnp.concatenate([f[1:], plane[None]], 0)


def before_x(f, plane):
    return jnp.concatenate([plane[None], f[:-1]], 0)


def packed(v):
    low, high = v[..., :HALF], v[..., HALF:]
    return jnp.where(lanes_of(low.shape) % DIRS < DIRS // 2, low, high)


def unpacked(v):
    near = lanes_of(v.shape) % DIRS < DIRS // 2
    axis = v.ndim - 1
    low = jnp.where(near, v, pltpu.roll(v, DIRS // 2, axis))
    high = jnp.where(near, pltpu.roll(v, HALF - DIRS // 2, axis), v)
    return jnp.concatenate([low, high], axis)


def put(buf, at, tangent, forward):
    n = len(tangent)
    for k in range(n):
        buf[at, 2 * k] = tangent[k][:, :HALF]
        buf[at, 2 * k + 1] = tangent[k][:, HALF:]
        buf[at, 2 * n + k] = packed(forward[k])


def take(buf, at, n):
    tangent = [jnp.concatenate([buf[at, 2 * k], buf[at, 2 * k + 1]], -1) for k in range(n)]
    forward = [unpacked(buf[at, 2 * n + k]) for k in range(n)]
    return (tangent, forward)


def sine(turn):
    u = turn * (2.0 * math.pi)
    s = u * u
    poly = -1.0 / 39916800.0
    for c in (1.0 / 362880.0, -1.0 / 5040.0, 1.0 / 120.0, -1.0 / 6.0):
        poly = poly * s + c
    return u + u * (s * poly)


def half_step_h(e, h, rim):
    ex, ey, ez = e
    hx, hy, hz = h
    xp, yp, xm, ym, cx, cy = rim
    new = (
        hx - time_step * ((after_rows(ez, yp[1][:, None, :]) - ez) - (next_z(ey) - ey)),
        hy - time_step * ((next_z(ex) - ex) - (after_x(ez, xp[1]) - ez)),
        hz - time_step * ((after_x(ey, xp[0]) - ey) - (after_rows(ex, yp[0][:, None, :]) - ex)),
    )
    x_y = xm[3] - time_step * ((next_z(xm[0]) - xm[0]) - (ez[0] - xm[2]))
    x_z = xm[4] - time_step * ((ey[0] - xm[1]) - (after_rows(xm[0], cx) - xm[0]))
    y_x = ym[3] - time_step * ((ez[:, 0, :] - ym[2]) - (next_z(ym[1]) - ym[1]))
    y_z = ym[4] - time_step * ((after_rows(ym[1], cy) - ym[1]) - (ex[:, 0, :] - ym[0]))
    return new, (x_y, x_z, y_x, y_z)


def curl_b(h, rim):
    hx, hy, hz = h
    x_y, x_z, y_x, y_z = rim
    return (
        (hz - before_rows(hz, y_z[:, None, :])) - (hy - prev_z(hy)),
        (hx - prev_z(hx)) - (hz - before_x(hz, x_z)),
        (hy - before_x(hy, x_y)) - (hx - before_rows(hx, y_x[:, None, :])),
    )


def widened(ref, lead):
    ny = ref.shape[-1]
    flat = LAYERS * ny
    total = 0.0
    for z in range(LAYERS):
        part = ref[..., z, :].reshape(lead, ny).astype(jnp.float32)
        place = (
            lax.broadcasted_iota(jnp.int32, (ny, flat), 1)
            == lax.broadcasted_iota(jnp.int32, (ny, flat), 0) + z * ny
        ).astype(jnp.float32)
        total = total + jnp.dot(part, place, precision=HIGHEST, preferred_element_type=jnp.float32)
    rows = jnp.broadcast_to(total[:, None, :], (lead, ny, flat))
    rows = jnp.where(lanes_of(rows.shape) % ny == sublanes_of(rows.shape), rows, 0.0)
    spread = (
        lax.broadcasted_iota(jnp.int32, (flat, WIDE), 0) // ny
        == lax.broadcasted_iota(jnp.int32, (flat, WIDE), 1) // DIRS
    ).astype(jnp.float32)
    wide = jnp.dot(
        rows.reshape(lead * ny, flat), spread, precision=HIGHEST, preferred_element_type=jnp.float32
    )
    return wide.reshape(lead, ny, WIDE)


def kernel(
    nx, ny, own,
    te, th, fe, fh, classes, material, permittivity, contrast, orders,
    out_e, out_h, out_s,
    s_xm, r_xm, s_xp, r_xp, s_ym, r_ym, s_yp, r_yp, s_cx, r_cx, s_cy, r_cy,
    gathered, partial, arrived, table_c, table_s,
    rim_send, rim_recv, g_send, g_recv, p_send, p_recv,
):
    wx, wy = te.shape[1], te.shape[2]
    i, j = lax.axis_index("gx"), lax.axis_index("gy")
    up, down = lax.rem(i + 1, nx), lax.rem(i + nx - 1, nx)
    right, left = lax.rem(j + 1, ny), lax.rem(j + ny - 1, ny)
    barrier = pltpu.get_barrier_semaphore()
    peers = [(lax.rem(i + d, nx), j) for d in range(1, nx)]
    peers += [(i, lax.rem(j + d, ny)) for d in range(1, ny)]
    peers += [(up, left), (down, right)]
    for peer in peers:
        pl.semaphore_signal(barrier, inc=1, device_id=peer, device_id_type=pl.DeviceIdType.MESH)

    def copy(src, dst, send, recv, device):
        return pltpu.make_async_remote_copy(
            src_ref=src, dst_ref=dst, send_sem=send, recv_sem=recv,
            device_id=device, device_id_type=pl.DeviceIdType.MESH,
        )

    def exchange(step, e, h, fe, fh):
        put(s_xm, step, [f[wx - 1] for f in (e[0], e[1], e[2], h[1], h[2])],
            [f[wx - 1] for f in (fe[0], fe[1], fe[2], fh[1], fh[2])])
        put(s_xp, step, [e[1][0], e[2][0]], [fe[1][0], fe[2][0]])
        put(s_ym, step, [f[:, wy - 1, :] for f in (e[0], e[1], e[2], h[0], h[2])],
            [f[:, wy - 1, :] for f in (fe[0], fe[1], fe[2], fh[0], fh[2])])
        put(s_yp, step, [e[0][:, 0, :], e[2][:, 0, :]], [fe[0][:, 0, :], fe[2][:, 0, :]])
        put(s_cx, step, [e[0][wx - 1, 0:1, :]], [fe[0][wx - 1, 0:1, :]])
        put(s_cy, step, [e[1][0, wy - 1:wy, :]], [fe[1][0, wy - 1:wy, :]])
        plan = (
            (s_xm, r_xm, (up, j)), (s_ym, r_ym, (i, right)), (s_xp, r_xp, (down, j)),
            (s_yp, r_yp, (i, left)), (s_cx, r_cx, (up, left)), (s_cy, r_cy, (down, right)),
        )
        if step == 0:
            pl.semaphore_wait(barrier, len(peers))
        copies = [
            copy(s.at[step], r.at[step], rim_send.at[step, k], rim_recv.at[step, k], device)
            for k, (s, r, device) in enumerate(plan)
        ]
        for c in copies:
            c.start()
        return copies

    e = [te[c] for c in range(3)]
    h = [th[c] for c in range(3)]
    wide_e = widened(fe, 3 * wx)
    wide_h = widened(fh, 3 * wx)
    fwd_e = [wide_e[c * wx:(c + 1) * wx] for c in range(3)]
    fwd_h = [wide_h[c * wx:(c + 1) * wx] for c in range(3)]
    waiting = exchange(0, e, h, fwd_e, fwd_h)

    kind = widened(material, wx)
    eps = jnp.zeros_like(kind)
    slope = jnp.zeros_like(kind)
    for k in range(permittivity.shape[0]):
        eps = jnp.where(kind == float(k), permittivity[k], eps)
        slope = jnp.where(kind == float(k), contrast[k], slope)
    inverse = time_step / eps
    coef = time_step * slope / (eps * eps)
    hot = widened(classes, wx) == (lanes_of(kind.shape) % DIRS).astype(jnp.float32)
    coef = jnp.where(hot, coef, 0.0)

    rows, cells = nx * own, ny * wx * wy
    count = orders.shape[1]
    row = lax.broadcasted_iota(jnp.int32, (rows, 1), 0)
    target = (row // own) * (ny * own) + j * own + row % own
    pick = (lax.broadcasted_iota(jnp.int32, (rows, count), 1) == target).astype(jnp.float32)
    pair = lax.dot_general(
        pick.astype(jnp.bfloat16), orders[...].astype(jnp.float32).astype(jnp.bfloat16),
        (((1,), (1,)), ((), ())), preferred_element_type=jnp.float32,
    )
    cell = lax.broadcasted_iota(jnp.int32, (1, cells), 1)
    all_x, all_y = nx * wx, ny * wy
    x_at = ((i * wx + (cell // wy) % wx) * all_y).astype(jnp.float32)
    y_at = (((cell // (wx * wy)) * wy + cell % wy) * all_x).astype(jnp.float32)
    index = pair[:, 0:1] * x_at + pair[:, 1:2] * y_at
    index = index - float(all_x * all_y) * jnp.round(index * (1.0 / (all_x * all_y)))
    turn = index * (1.0 / (all_x * all_y))
    table_c[...] = sine(0.25 - jnp.abs(turn))
    table_s[...] = sine(jnp.where(turn > 0.25, 0.5 - turn, jnp.where(turn < -0.25, -0.5 - turn, turn)))

    for step in range(STEPS):
        for c in waiting:
            c.wait()
        xm, ym = take(r_xm, step, 5), take(r_ym, step, 5)
        xp, yp = take(r_xp, step, 2), take(r_yp, step, 2)
        cx, cy = take(r_cx, step, 1), take(r_cy, step, 1)
        fwd_h, rim = half_step_h(fwd_e, fwd_h, (xp[1], yp[1], xm[1], ym[1], cx[1][0], cy[1][0]))
        fwd_c = curl_b(fwd_h, rim)
        fwd_e = [fwd_e[c] + inverse * fwd_c[c] for c in range(3)]
        h, rim = half_step_h(e, h, (xp[0], yp[0], xm[0], ym[0], cx[0][0], cy[0][0]))
        tan_c = curl_b(h, rim)
        e = [e[c] + inverse * tan_c[c] - coef * fwd_c[c] for c in range(3)]
        if step < STEPS - 1:
            waiting = exchange(step + 1, e, h, fwd_e, fwd_h)

    top_x, top_y = e[0][:, :, HALF:], e[1][:, :, HALF:]
    top = jnp.where(lanes_of(top_x.shape) < DIRS, pltpu.roll(top_x, DIRS, 2), top_y)
    gathered[j] = top.reshape(wx * wy, 2 * DIRS)
    copies = [
        copy(gathered.at[j], gathered.at[j], g_send.at[d], g_recv.at[d], (i, lax.rem(j + d, ny)))
        for d in range(1, ny)
    ]
    for c in copies:
        c.start()
    for c in range(3):
        out_e[c] = e[c]
        out_h[c] = h[c]
    for c in copies:
        c.wait()
    every = gathered[...].reshape(cells, 2 * DIRS)
    real = jnp.dot(table_c[...], every, precision=HIGHEST, preferred_element_type=jnp.float32)
    imag = jnp.dot(table_s[...], every, precision=HIGHEST, preferred_element_type=jnp.float32)
    for k in range(nx):
        partial[k, 0] = real[k * own:(k + 1) * own]
        partial[k, 1] = imag[k * own:(k + 1) * own]
    copies = []
    for d in range(1, nx):
        peer = lax.rem(i + d, nx)
        copies.append(copy(partial.at[peer], arrived.at[d - 1], p_send.at[d], p_recv.at[d], (peer, j)))
    for c in copies:
        c.start()
    total = partial[i]
    for c in copies:
        c.wait()
    for d in range(nx - 1):
        total = total + arrived[d]
    scale = 1.0 / math.sqrt(all_x * all_y)
    re, im = total[0] * scale, total[1] * -scale
    low = lanes_of(re.shape) < DIRS
    out_s[:, :2 * DIRS] = jnp.where(low, re, pltpu.roll(im, DIRS, 1))
    out_s[:, 2 * DIRS:] = jnp.where(low, pltpu.roll(re, DIRS, 1), im)


def local(nx, ny, te, th, fe, fh, classes, material, permittivity, contrast, orders):
    wx, wy = te.shape[1], te.shape[2]
    own = orders.shape[0] // (nx * ny)
    rows, cells = nx * own, ny * wx * wy
    f32 = jnp.float32
    vmem = pl.BlockSpec(memory_space=pltpu.VMEM)
    smem = pl.BlockSpec(memory_space=pltpu.SMEM)

    def two(*shape):
        return [pltpu.VMEM((STEPS,) + shape, f32)] * 2

    return pl.pallas_call(
        functools.partial(kernel, nx, ny, own),
        out_shape=(
            jax.ShapeDtypeStruct(te.shape, f32),
            jax.ShapeDtypeStruct(th.shape, f32),
            jax.ShapeDtypeStruct((own, 4 * DIRS), f32),
        ),
        in_specs=[vmem] * 6 + [smem] * 2 + [vmem],
        out_specs=(vmem, vmem, vmem),
        scratch_shapes=[
            *two(15, wy, HALF), *two(6, wy, HALF), *two(15, wx, HALF), *two(6, wx, HALF),
            *two(3, 1, HALF), *two(3, 1, HALF),
            pltpu.VMEM((ny, wx * wy, 2 * DIRS), f32),
            pltpu.VMEM((nx, 2, own, 2 * DIRS), f32),
            pltpu.VMEM((nx - 1, 2, own, 2 * DIRS), f32),
            pltpu.VMEM((rows, cells), f32),
            pltpu.VMEM((rows, cells), f32),
            pltpu.SemaphoreType.DMA((STEPS, 6)), pltpu.SemaphoreType.DMA((STEPS, 6)),
            pltpu.SemaphoreType.DMA((ny,)), pltpu.SemaphoreType.DMA((ny,)),
            pltpu.SemaphoreType.DMA((nx,)), pltpu.SemaphoreType.DMA((nx,)),
        ],
        compiler_params=pltpu.CompilerParams(
            collective_id=0, has_side_effects=True, vmem_limit_bytes=40 * 1024 * 1024
        ),
        name="slab",
    )(
        te, th, jnp.transpose(fe, (0, 1, 3, 2)), jnp.transpose(fh, (0, 1, 3, 2)),
        jnp.transpose(classes, (0, 2, 1)), jnp.transpose(material, (0, 2, 1)),
        permittivity, contrast, jnp.transpose(orders),
    )


def solution(mesh):
    in_specs = (
        P(None, "gx", "gy", None),
        P(None, "gx", "gy", None),
        P(None, "gx", "gy", None),
        P(None, "gx", "gy", None),
        P("gx", "gy", None),
        P("gx", "gy", None),
        P(),
        P(),
        P(),
    )
    out_specs = (P(None, "gx", "gy", None), P(None, "gx", "gy", None), P(("gx", "gy"), None))
    body = functools.partial(local, mesh.shape["gx"], mesh.shape["gy"])
    return jax.shard_map(body, mesh=mesh, in_specs=in_specs, out_specs=out_specs, check_vma=False)
```

```python
import functools
import math

import jax
import jax.numpy as jnp
from jax import lax
from jax.experimental import pallas as pl
from jax.experimental.pallas import tpu as pltpu
from jax.sharding import PartitionSpec as P

DIRS = 64
STEPS = 2
LAYERS = 4
WIDE = LAYERS * DIRS
HALF = WIDE // 2
time_step = 0.5


def lanes_of(shape):
    return lax.broadcasted_iota(jnp.int32, shape, len(shape) - 1)


def sublanes_of(shape):
    return lax.broadcasted_iota(jnp.int32, shape, len(shape) - 2)


def next_z(f):
    return jnp.where(lanes_of(f.shape) < WIDE - DIRS, pltpu.roll(f, WIDE - DIRS, f.ndim - 1), 0.0)


def prev_z(f):
    return jnp.where(lanes_of(f.shape) >= DIRS, pltpu.roll(f, DIRS, f.ndim - 1), 0.0)


def after_rows(f, row):
    n = f.shape[-2]
    return jnp.where(sublanes_of(f.shape) == n - 1, row, pltpu.roll(f, n - 1, f.ndim - 2))


def before_rows(f, row):
    return jnp.where(sublanes_of(f.shape) == 0, row, pltpu.roll(f, 1, f.ndim - 2))


def after_x(f, plane):
    return jnp.concatenate([f[1:], plane[None]], 0)


def before_x(f, plane):
    return jnp.concatenate([plane[None], f[:-1]], 0)


def packed(v):
    low, high = v[..., :HALF], v[..., HALF:]
    return jnp.where(lanes_of(low.shape) % DIRS < DIRS // 2, low, high)


def unpacked(v):
    near = lanes_of(v.shape) % DIRS < DIRS // 2
    axis = v.ndim - 1
    low = jnp.where(near, v, pltpu.roll(v, DIRS // 2, axis))
    high = jnp.where(near, pltpu.roll(v, HALF - DIRS // 2, axis), v)
    return jnp.concatenate([low, high], axis)


def take(buf, at, n):
    tangent = [jnp.concatenate([buf[at, 2 * k], buf[at, 2 * k + 1]], -1) for k in range(n)]
    forward = [unpacked(buf[at, 2 * n + k]) for k in range(n)]
    return (tangent, forward)


def sine(turn):
    u = turn * (2.0 * math.pi)
    s = u * u
    poly = -1.0 / 39916800.0
    for c in (1.0 / 362880.0, -1.0 / 5040.0, 1.0 / 120.0, -1.0 / 6.0):
        poly = poly * s + c
    return u + u * (s * poly)


def half_step_h(e, h, rim):
    ex, ey, ez = e
    hx, hy, hz = h
    xp, yp, xm, ym, cx, cy = rim
    new = (
        hx - time_step * ((after_rows(ez, yp[1][:, None, :]) - ez) - (next_z(ey) - ey)),
        hy - time_step * ((next_z(ex) - ex) - (after_x(ez, xp[1]) - ez)),
        hz - time_step * ((after_x(ey, xp[0]) - ey) - (after_rows(ex, yp[0][:, None, :]) - ex)),
    )
    x_y = xm[3] - time_step * ((next_z(xm[0]) - xm[0]) - (ez[0] - xm[2]))
    x_z = xm[4] - time_step * ((ey[0] - xm[1]) - (after_rows(xm[0], cx) - xm[0]))
    y_x = ym[3] - time_step * ((ez[:, 0, :] - ym[2]) - (next_z(ym[1]) - ym[1]))
    y_z = ym[4] - time_step * ((after_rows(ym[1], cy) - ym[1]) - (ex[:, 0, :] - ym[0]))
    return new, (x_y, x_z, y_x, y_z)


def curl_b(h, rim):
    hx, hy, hz = h
    x_y, x_z, y_x, y_z = rim
    return (
        (hz - before_rows(hz, y_z[:, None, :])) - (hy - prev_z(hy)),
        (hx - prev_z(hx)) - (hz - before_x(hz, x_z)),
        (hy - before_x(hy, x_y)) - (hx - before_rows(hx, y_x[:, None, :])),
    )


def split(v):
    parts = []
    for _ in range(3):
        parts.append(v.astype(jnp.bfloat16))
        v = v - parts[-1].astype(jnp.float32)
    return parts


def widened(layers, ny):
    lead = layers[0].shape[0]
    flat = LAYERS * ny
    total = 0.0
    for z in range(LAYERS):
        for k, part in enumerate(split(layers[z])):
            place = (
                lax.broadcasted_iota(jnp.int32, (ny, 3 * flat), 1)
                == lax.broadcasted_iota(jnp.int32, (ny, 3 * flat), 0) + (k * flat + z * ny)
            ).astype(jnp.float32)
            total = total + jnp.dot(part, place.astype(jnp.bfloat16), preferred_element_type=jnp.float32)
    rows = jnp.broadcast_to(total[:, None, :], (lead, ny, 3 * flat))
    rows = jnp.where(lanes_of(rows.shape) % ny == sublanes_of(rows.shape), rows, 0.0)
    spread = (
        (lax.broadcasted_iota(jnp.int32, (3 * flat, WIDE), 0) // ny) % LAYERS
        == lax.broadcasted_iota(jnp.int32, (3 * flat, WIDE), 1) // DIRS
    ).astype(jnp.float32)
    wide = jnp.dot(
        rows.reshape(lead * ny, 3 * flat).astype(jnp.bfloat16),
        spread.astype(jnp.bfloat16),
        preferred_element_type=jnp.float32,
    )
    return wide.reshape(lead, ny, WIDE)


def kernel(
    nx, ny, own,
    te_at, th_at, fe_at, fh_at, classes_at, material_at, permittivity_at, contrast_at, orders_at,
    out_e, out_h, out_s,
    s_xm, r_xm, s_xp, r_xp, s_ym, r_ym, s_yp, r_yp, s_cx, r_cx, s_cy, r_cy,
    gathered, partial, arrived, table_c, table_s,
    rim_send, rim_recv, g_send, g_recv, p_send, p_recv,
    te, th, fe, fh, classes, material, permittivity, contrast, orders, load,
):
    loads = [
        pltpu.make_async_copy(src, dst, load.at[k])
        for k, (src, dst) in enumerate((
            (te_at, te), (th_at, th), (fe_at, fe), (fh_at, fh), (classes_at, classes),
            (material_at, material), (permittivity_at, permittivity), (contrast_at, contrast),
            (orders_at, orders),
        ))
    ]
    for c in loads:
        c.start()
    wx, wy = te.shape[1], te.shape[2]
    i, j = lax.axis_index("gx"), lax.axis_index("gy")
    up, down = lax.rem(i + 1, nx), lax.rem(i + nx - 1, nx)
    right, left = lax.rem(j + 1, ny), lax.rem(j + ny - 1, ny)
    barrier = pltpu.get_barrier_semaphore()
    peers = [(lax.rem(i + d, nx), j) for d in range(1, nx)]
    peers += [(i, lax.rem(j + d, ny)) for d in range(1, ny)]
    peers += [(up, left), (down, right)]
    for peer in peers:
        pl.semaphore_signal(barrier, inc=1, device_id=peer, device_id_type=pl.DeviceIdType.MESH)

    def copy(src, dst, send, recv, device):
        return pltpu.make_async_remote_copy(
            src_ref=src, dst_ref=dst, send_sem=send, recv_sem=recv,
            device_id=device, device_id_type=pl.DeviceIdType.MESH,
        )

    def planes_of(e, h):
        return (
            [f[wx - 1] for f in (e[0], e[1], e[2], h[1], h[2])],
            [f[:, wy - 1, :] for f in (e[0], e[1], e[2], h[0], h[2])],
            [e[1][0], e[2][0]],
            [e[0][:, 0, :], e[2][:, 0, :]],
            [e[0][wx - 1, 0:1, :]],
            [e[1][0, wy - 1:wy, :]],
        )

    rims = (
        (s_xm, r_xm, (up, j)), (s_ym, r_ym, (i, right)), (s_xp, r_xp, (down, j)),
        (s_yp, r_yp, (i, left)), (s_cx, r_cx, (up, left)), (s_cy, r_cy, (down, right)),
    )

    def put_tangent(step, e, h):
        for (buf, _, _), planes in zip(rims, planes_of(e, h)):
            for k, plane in enumerate(planes):
                buf[step, 2 * k] = plane[:, :HALF]
                buf[step, 2 * k + 1] = plane[:, HALF:]

    def put_forward(step, e, h):
        for (buf, _, _), planes in zip(rims, planes_of(e, h)):
            for k, plane in enumerate(planes):
                buf[step, 2 * len(planes) + k] = packed(plane)

    def send(step, first, part):
        copies = []
        for k, (s, r, device) in enumerate(rims):
            n = s.shape[1] // 3
            span = (pl.ds(0, 3 * n), pl.ds(0, 2 * n), pl.ds(2 * n, n))[part]
            copies.append(copy(
                s.at[step, span], r.at[step, span], rim_send.at[first + k], rim_recv.at[first + k], device
            ))
        for c in copies:
            c.start()
        return copies

    for c in loads[:2]:
        c.wait()
    e = [te[c] for c in range(3)]
    h = [th[c] for c in range(3)]
    put_tangent(0, e, h)
    pl.semaphore_wait(barrier, len(peers))
    waiting = send(0, 0, 1)
    for c in loads[2:]:
        c.wait()
    layers = []
    for z in range(LAYERS):
        layers.append(jnp.concatenate([
            fe[:, :, z, :].reshape(3 * wx, wy), fh[:, :, z, :].reshape(3 * wx, wy),
            classes[:, z, :].astype(jnp.float32), material[:, z, :].astype(jnp.float32),
        ], 0))
    wide = widened(layers, wy)
    fwd_e = [wide[c * wx:(c + 1) * wx] for c in range(3)]
    fwd_h = [wide[c * wx:(c + 1) * wx] for c in range(3, 6)]
    put_forward(0, fwd_e, fwd_h)
    waiting += send(0, 6, 2)

    kind = wide[7 * wx:]
    eps = jnp.zeros_like(kind)
    slope = jnp.zeros_like(kind)
    for k in range(permittivity.shape[0]):
        eps = jnp.where(kind == float(k), permittivity[k], eps)
        slope = jnp.where(kind == float(k), contrast[k], slope)
    inverse = time_step / eps
    coef = time_step * slope / (eps * eps)
    hot = wide[6 * wx:7 * wx] == (lanes_of(kind.shape) % DIRS).astype(jnp.float32)
    coef = jnp.where(hot, coef, 0.0)

    rows, cells = nx * own, ny * wx * wy
    count = orders.shape[1]
    row = lax.broadcasted_iota(jnp.int32, (rows, 1), 0)
    target = (row // own) * (ny * own) + j * own + row % own
    pick = (lax.broadcasted_iota(jnp.int32, (rows, count), 1) == target).astype(jnp.float32)
    pair = lax.dot_general(
        pick.astype(jnp.bfloat16), orders[...].astype(jnp.float32).astype(jnp.bfloat16),
        (((1,), (1,)), ((), ())), preferred_element_type=jnp.float32,
    )
    cell = lax.broadcasted_iota(jnp.int32, (1, cells), 1)
    all_x, all_y = nx * wx, ny * wy
    x_at = ((i * wx + (cell // wy) % wx) * all_y).astype(jnp.float32)
    y_at = (((cell // (wx * wy)) * wy + cell % wy) * all_x).astype(jnp.float32)
    index = pair[:, 0:1] * x_at + pair[:, 1:2] * y_at
    index = index - float(all_x * all_y) * jnp.round(index * (1.0 / (all_x * all_y)))
    turn = index * (1.0 / (all_x * all_y))
    cosine = sine(0.25 - jnp.abs(turn))
    sines = sine(jnp.where(turn > 0.25, 0.5 - turn, jnp.where(turn < -0.25, -0.5 - turn, turn)))
    for table, value in ((table_c, cosine), (table_s, sines)):
        near, far = split(value)[:2]
        table[:, :cells] = near
        table[:, cells:2 * cells] = far
        table[:, 2 * cells:] = near

    for step in range(STEPS):
        for c in waiting:
            c.wait()
        xm, ym = take(r_xm, step, 5), take(r_ym, step, 5)
        xp, yp = take(r_xp, step, 2), take(r_yp, step, 2)
        cx, cy = take(r_cx, step, 1), take(r_cy, step, 1)
        fwd_h, rim = half_step_h(fwd_e, fwd_h, (xp[1], yp[1], xm[1], ym[1], cx[1][0], cy[1][0]))
        fwd_c = curl_b(fwd_h, rim)
        fwd_e = [fwd_e[c] + inverse * fwd_c[c] for c in range(3)]
        h, rim = half_step_h(e, h, (xp[0], yp[0], xm[0], ym[0], cx[0][0], cy[0][0]))
        tan_c = curl_b(h, rim)
        e = [e[c] + inverse * tan_c[c] - coef * fwd_c[c] for c in range(3)]
        if step < STEPS - 1:
            put_tangent(step + 1, e, h)
            put_forward(step + 1, fwd_e, fwd_h)
            waiting = send(step + 1, 12 + 6 * step, 0)

    top_x, top_y = e[0][:, :, HALF:], e[1][:, :, HALF:]
    top = jnp.where(lanes_of(top_x.shape) < DIRS, pltpu.roll(top_x, DIRS, 2), top_y)
    gathered[j] = top.reshape(wx * wy, 2 * DIRS)
    copies = [
        copy(gathered.at[j], gathered.at[j], g_send.at[d], g_recv.at[d], (i, lax.rem(j + d, ny)))
        for d in range(1, ny)
    ]
    for c in copies:
        c.start()
    for c in range(3):
        out_e[c] = e[c]
        out_h[c] = h[c]
    for c in copies:
        c.wait()
    every = gathered[...].reshape(cells, 2 * DIRS)
    near, far = split(every)[:2]
    every = jnp.concatenate([near, near, far], 0)
    real = jnp.dot(table_c[...], every, preferred_element_type=jnp.float32)
    imag = jnp.dot(table_s[...], every, preferred_element_type=jnp.float32)
    for k in range(nx):
        partial[k, 0] = real[k * own:(k + 1) * own]
        partial[k, 1] = imag[k * own:(k + 1) * own]
    copies = []
    for d in range(1, nx):
        peer = lax.rem(i + d, nx)
        copies.append(copy(partial.at[peer], arrived.at[d - 1], p_send.at[d], p_recv.at[d], (peer, j)))
    for c in copies:
        c.start()
    total = partial[i]
    for c in copies:
        c.wait()
    for d in range(nx - 1):
        total = total + arrived[d]
    scale = 1.0 / math.sqrt(all_x * all_y)
    re, im = total[0] * scale, total[1] * -scale
    low = lanes_of(re.shape) < DIRS
    out_s[:, :2 * DIRS] = jnp.where(low, re, pltpu.roll(im, DIRS, 1))
    out_s[:, 2 * DIRS:] = jnp.where(low, pltpu.roll(re, DIRS, 1), im)


def local(nx, ny, te, th, fe, fh, classes, material, permittivity, contrast, orders):
    wx, wy = te.shape[1], te.shape[2]
    own = orders.shape[0] // (nx * ny)
    rows, cells = nx * own, ny * wx * wy
    f32 = jnp.float32
    vmem = pl.BlockSpec(memory_space=pltpu.VMEM)
    args = (
        te, th, jnp.transpose(fe, (0, 1, 3, 2)), jnp.transpose(fh, (0, 1, 3, 2)),
        jnp.transpose(classes, (0, 2, 1)), jnp.transpose(material, (0, 2, 1)),
        permittivity, contrast, jnp.transpose(orders),
    )

    def two(*shape):
        return [pltpu.VMEM((STEPS,) + shape, f32)] * 2

    return pl.pallas_call(
        functools.partial(kernel, nx, ny, own),
        out_shape=(
            jax.ShapeDtypeStruct(te.shape, f32),
            jax.ShapeDtypeStruct(th.shape, f32),
            jax.ShapeDtypeStruct((own, 4 * DIRS), f32),
        ),
        in_specs=[pl.BlockSpec(memory_space=pltpu.HBM)] * 9,
        out_specs=(vmem, vmem, vmem),
        scratch_shapes=[
            *two(15, wy, HALF), *two(6, wy, HALF), *two(15, wx, HALF), *two(6, wx, HALF),
            *two(3, 1, HALF), *two(3, 1, HALF),
            pltpu.VMEM((ny, wx * wy, 2 * DIRS), f32),
            pltpu.VMEM((nx, 2, own, 2 * DIRS), f32),
            pltpu.VMEM((nx - 1, 2, own, 2 * DIRS), f32),
            pltpu.VMEM((rows, 3 * cells), jnp.bfloat16),
            pltpu.VMEM((rows, 3 * cells), jnp.bfloat16),
            pltpu.SemaphoreType.DMA((6 * STEPS + 6,)), pltpu.SemaphoreType.DMA((6 * STEPS + 6,)),
            pltpu.SemaphoreType.DMA((ny,)), pltpu.SemaphoreType.DMA((ny,)),
            pltpu.SemaphoreType.DMA((nx,)), pltpu.SemaphoreType.DMA((nx,)),
            *[pltpu.VMEM(v.shape, v.dtype) for v in args[:6]],
            *[pltpu.SMEM(v.shape, v.dtype) for v in args[6:8]],
            pltpu.VMEM(args[8].shape, args[8].dtype),
            pltpu.SemaphoreType.DMA((9,)),
        ],
        compiler_params=pltpu.CompilerParams(
            collective_id=0, has_side_effects=True, vmem_limit_bytes=64 * 1024 * 1024 - 65536
        ),
        name="slab",
    )(*args)


def solution(mesh):
    in_specs = (
        P(None, "gx", "gy", None),
        P(None, "gx", "gy", None),
        P(None, "gx", "gy", None),
        P(None, "gx", "gy", None),
        P("gx", "gy", None),
        P("gx", "gy", None),
        P(),
        P(),
        P(),
    )
    out_specs = (P(None, "gx", "gy", None), P(None, "gx", "gy", None), P(("gx", "gy"), None))
    body = functools.partial(local, mesh.shape["gx"], mesh.shape["gy"])
    return jax.shard_map(body, mesh=mesh, in_specs=in_specs, out_specs=out_specs, check_vma=False)
```

```python
import functools
import math

import jax
import jax.numpy as jnp
from jax import lax
from jax.experimental import pallas as pl
from jax.experimental.pallas import tpu as pltpu
from jax.sharding import PartitionSpec as P

DIRS = 64
STEPS = 2
LAYERS = 4
WIDE = LAYERS * DIRS
HALF = WIDE // 2
time_step = 0.5


def lanes_of(shape):
    return lax.broadcasted_iota(jnp.int32, shape, len(shape) - 1)


def sublanes_of(shape):
    return lax.broadcasted_iota(jnp.int32, shape, len(shape) - 2)


def next_z(f):
    return jnp.where(lanes_of(f.shape) < WIDE - DIRS, pltpu.roll(f, WIDE - DIRS, f.ndim - 1), 0.0)


def prev_z(f):
    return jnp.where(lanes_of(f.shape) >= DIRS, pltpu.roll(f, DIRS, f.ndim - 1), 0.0)


def after_rows(f, row):
    n = f.shape[-2]
    return jnp.where(sublanes_of(f.shape) == n - 1, row, pltpu.roll(f, n - 1, f.ndim - 2))


def before_rows(f, row):
    return jnp.where(sublanes_of(f.shape) == 0, row, pltpu.roll(f, 1, f.ndim - 2))


def after_x(f, plane):
    return jnp.concatenate([f[1:], plane[None]], 0)


def before_x(f, plane):
    return jnp.concatenate([plane[None], f[:-1]], 0)


def packed(v):
    low, high = v[..., :HALF], v[..., HALF:]
    return jnp.where(lanes_of(low.shape) % DIRS < DIRS // 2, low, high)


def unpacked(v):
    near = lanes_of(v.shape) % DIRS < DIRS // 2
    axis = v.ndim - 1
    low = jnp.where(near, v, pltpu.roll(v, DIRS // 2, axis))
    high = jnp.where(near, pltpu.roll(v, HALF - DIRS // 2, axis), v)
    return jnp.concatenate([low, high], axis)


def take(buf, at, n):
    tangent = [jnp.concatenate([buf[at, 2 * k], buf[at, 2 * k + 1]], -1) for k in range(n)]
    forward = [unpacked(buf[at, 2 * n + k]) for k in range(n)]
    return (tangent, forward)


def sine(turn):
    u = turn * (2.0 * math.pi)
    s = u * u
    poly = -1.0 / 39916800.0
    for c in (1.0 / 362880.0, -1.0 / 5040.0, 1.0 / 120.0, -1.0 / 6.0):
        poly = poly * s + c
    return u + u * (s * poly)


def half_step_h(e, h, rim):
    ex, ey, ez = e
    hx, hy, hz = h
    xp, yp, xm, ym, cx, cy = rim
    new = (
        hx - time_step * ((after_rows(ez, yp[1][:, None, :]) - ez) - (next_z(ey) - ey)),
        hy - time_step * ((next_z(ex) - ex) - (after_x(ez, xp[1]) - ez)),
        hz - time_step * ((after_x(ey, xp[0]) - ey) - (after_rows(ex, yp[0][:, None, :]) - ex)),
    )
    x_y = xm[3] - time_step * ((next_z(xm[0]) - xm[0]) - (ez[0] - xm[2]))
    x_z = xm[4] - time_step * ((ey[0] - xm[1]) - (after_rows(xm[0], cx) - xm[0]))
    y_x = ym[3] - time_step * ((ez[:, 0, :] - ym[2]) - (next_z(ym[1]) - ym[1]))
    y_z = ym[4] - time_step * ((after_rows(ym[1], cy) - ym[1]) - (ex[:, 0, :] - ym[0]))
    return new, (x_y, x_z, y_x, y_z)


def curl_b(h, rim):
    hx, hy, hz = h
    x_y, x_z, y_x, y_z = rim
    return (
        (hz - before_rows(hz, y_z[:, None, :])) - (hy - prev_z(hy)),
        (hx - prev_z(hx)) - (hz - before_x(hz, x_z)),
        (hy - before_x(hy, x_y)) - (hx - before_rows(hx, y_x[:, None, :])),
    )


def split(v):
    parts = []
    for _ in range(3):
        parts.append(v.astype(jnp.bfloat16))
        v = v - parts[-1].astype(jnp.float32)
    return parts


def widened(layers, ny):
    lead = layers[0].shape[0]
    flat = LAYERS * ny
    total = 0.0
    for z in range(LAYERS):
        for k, part in enumerate(split(layers[z])):
            place = (
                lax.broadcasted_iota(jnp.int32, (ny, 3 * flat), 1)
                == lax.broadcasted_iota(jnp.int32, (ny, 3 * flat), 0) + (k * flat + z * ny)
            ).astype(jnp.float32)
            total = total + jnp.dot(part, place.astype(jnp.bfloat16), preferred_element_type=jnp.float32)
    rows = jnp.broadcast_to(total[:, None, :], (lead, ny, 3 * flat))
    rows = jnp.where(lanes_of(rows.shape) % ny == sublanes_of(rows.shape), rows, 0.0)
    spread = (
        (lax.broadcasted_iota(jnp.int32, (3 * flat, WIDE), 0) // ny) % LAYERS
        == lax.broadcasted_iota(jnp.int32, (3 * flat, WIDE), 1) // DIRS
    ).astype(jnp.float32)
    wide = jnp.dot(
        rows.reshape(lead * ny, 3 * flat).astype(jnp.bfloat16),
        spread.astype(jnp.bfloat16),
        preferred_element_type=jnp.float32,
    )
    return wide.reshape(lead, ny, WIDE)


def kernel(
    nx, ny, own,
    te_at, th_at, fe_at, fh_at, classes_at, material_at, permittivity_at, contrast_at, orders_at,
    out_e, out_h, out_s,
    s_xm, r_xm, s_xp, r_xp, s_ym, r_ym, s_yp, r_yp, s_cx, r_cx, s_cy, r_cy,
    gathered, partial, paired, summed, arrived, table_c, table_s,
    rim_send, rim_recv, g_send, g_recv, p_send, p_recv,
    te, th, fe, fh, classes, material, permittivity, contrast, orders, load, new_e, new_h, store,
):
    loads = [
        pltpu.make_async_copy(src, dst, load.at[k])
        for k, (src, dst) in enumerate((
            (te_at, te), (th_at, th), (fe_at, fe), (fh_at, fh), (classes_at, classes),
            (material_at, material), (permittivity_at, permittivity), (contrast_at, contrast),
            (orders_at, orders),
        ))
    ]
    for c in loads:
        c.start()
    wx, wy = te.shape[1], te.shape[2]
    i, j = lax.axis_index("gx"), lax.axis_index("gy")
    up, down = lax.rem(i + 1, nx), lax.rem(i + nx - 1, nx)
    right, left = lax.rem(j + 1, ny), lax.rem(j + ny - 1, ny)
    barrier = pltpu.get_barrier_semaphore()
    offsets = sorted({1, nx - 1, *range(2, nx, 2)})
    peers = [(lax.rem(i + d, nx), j) for d in offsets]
    peers += [(i, lax.rem(j + d, ny)) for d in range(1, ny)]
    peers += [(up, left), (down, right)]
    for peer in peers:
        pl.semaphore_signal(barrier, inc=1, device_id=peer, device_id_type=pl.DeviceIdType.MESH)

    def copy(src, dst, send, recv, device):
        return pltpu.make_async_remote_copy(
            src_ref=src, dst_ref=dst, send_sem=send, recv_sem=recv,
            device_id=device, device_id_type=pl.DeviceIdType.MESH,
        )

    def planes_of(e, h):
        return (
            [f[wx - 1] for f in (e[0], e[1], e[2], h[1], h[2])],
            [f[:, wy - 1, :] for f in (e[0], e[1], e[2], h[0], h[2])],
            [e[1][0], e[2][0]],
            [e[0][:, 0, :], e[2][:, 0, :]],
            [e[0][wx - 1, 0:1, :]],
            [e[1][0, wy - 1:wy, :]],
        )

    rims = (
        (s_xm, r_xm, (up, j)), (s_ym, r_ym, (i, right)), (s_xp, r_xp, (down, j)),
        (s_yp, r_yp, (i, left)), (s_cx, r_cx, (up, left)), (s_cy, r_cy, (down, right)),
    )

    def put_tangent(step, e, h):
        for (buf, _, _), planes in zip(rims, planes_of(e, h)):
            for k, plane in enumerate(planes):
                buf[step, 2 * k] = plane[:, :HALF]
                buf[step, 2 * k + 1] = plane[:, HALF:]

    def put_forward(step, e, h):
        for (buf, _, _), planes in zip(rims, planes_of(e, h)):
            for k, plane in enumerate(planes):
                buf[step, 2 * len(planes) + k] = packed(plane)

    def send(step, first, part):
        copies = []
        for k, (s, r, device) in enumerate(rims):
            n = s.shape[1] // 3
            span = (pl.ds(0, 3 * n), pl.ds(0, 2 * n), pl.ds(2 * n, n))[part]
            copies.append(copy(
                s.at[step, span], r.at[step, span], rim_send.at[first + k], rim_recv.at[first + k], device
            ))
        for c in copies:
            c.start()
        return copies

    for c in loads[:2]:
        c.wait()
    e = [te[c] for c in range(3)]
    h = [th[c] for c in range(3)]
    put_tangent(0, e, h)
    pl.semaphore_wait(barrier, len(peers))
    waiting = send(0, 0, 1)
    for c in loads[2:]:
        c.wait()
    layers = []
    for z in range(LAYERS):
        layers.append(jnp.concatenate([
            fe[:, :, z, :].reshape(3 * wx, wy), fh[:, :, z, :].reshape(3 * wx, wy),
            classes[:, z, :].astype(jnp.float32), material[:, z, :].astype(jnp.float32),
        ], 0))
    wide = widened(layers, wy)
    fwd_e = [wide[c * wx:(c + 1) * wx] for c in range(3)]
    fwd_h = [wide[c * wx:(c + 1) * wx] for c in range(3, 6)]
    put_forward(0, fwd_e, fwd_h)
    waiting += send(0, 6, 2)

    kind = wide[7 * wx:]
    eps = jnp.zeros_like(kind)
    slope = jnp.zeros_like(kind)
    for k in range(permittivity.shape[0]):
        eps = jnp.where(kind == float(k), permittivity[k], eps)
        slope = jnp.where(kind == float(k), contrast[k], slope)
    inverse = time_step / eps
    coef = time_step * slope / (eps * eps)
    hot = wide[6 * wx:7 * wx] == (lanes_of(kind.shape) % DIRS).astype(jnp.float32)
    coef = jnp.where(hot, coef, 0.0)

    rows, cells = nx * own, ny * wx * wy
    count = orders.shape[1]
    row = lax.broadcasted_iota(jnp.int32, (rows, 1), 0)
    target = (row // own) * (ny * own) + j * own + row % own
    pick = (lax.broadcasted_iota(jnp.int32, (rows, count), 1) == target).astype(jnp.float32)
    pair = lax.dot_general(
        pick.astype(jnp.bfloat16), orders[...].astype(jnp.float32).astype(jnp.bfloat16),
        (((1,), (1,)), ((), ())), preferred_element_type=jnp.float32,
    )
    cell = lax.broadcasted_iota(jnp.int32, (1, cells), 1)
    all_x, all_y = nx * wx, ny * wy
    x_at = ((i * wx + (cell // wy) % wx) * all_y).astype(jnp.float32)
    y_at = (((cell // (wx * wy)) * wy + cell % wy) * all_x).astype(jnp.float32)
    index = pair[:, 0:1] * x_at + pair[:, 1:2] * y_at
    index = index - float(all_x * all_y) * jnp.round(index * (1.0 / (all_x * all_y)))
    turn = index * (1.0 / (all_x * all_y))
    cosine = sine(0.25 - jnp.abs(turn))
    sines = sine(jnp.where(turn > 0.25, 0.5 - turn, jnp.where(turn < -0.25, -0.5 - turn, turn)))
    for table, value in ((table_c, cosine), (table_s, sines)):
        near, far = split(value)[:2]
        table[:, :cells] = near
        table[:, cells:2 * cells] = far
        table[:, 2 * cells:] = near

    for step in range(STEPS):
        for c in waiting:
            c.wait()
        xm, ym = take(r_xm, step, 5), take(r_ym, step, 5)
        xp, yp = take(r_xp, step, 2), take(r_yp, step, 2)
        cx, cy = take(r_cx, step, 1), take(r_cy, step, 1)
        fwd_h, rim = half_step_h(fwd_e, fwd_h, (xp[1], yp[1], xm[1], ym[1], cx[1][0], cy[1][0]))
        fwd_c = curl_b(fwd_h, rim)
        fwd_e = [fwd_e[c] + inverse * fwd_c[c] for c in range(3)]
        h, rim = half_step_h(e, h, (xp[0], yp[0], xm[0], ym[0], cx[0][0], cy[0][0]))
        tan_c = curl_b(h, rim)
        e = [e[c] + inverse * tan_c[c] - coef * fwd_c[c] for c in range(3)]
        if step < STEPS - 1:
            put_tangent(step + 1, e, h)
            put_forward(step + 1, fwd_e, fwd_h)
            waiting = send(step + 1, 12 + 6 * step, 0)

    top_x, top_y = e[0][:, :, HALF:], e[1][:, :, HALF:]
    top = jnp.where(lanes_of(top_x.shape) < DIRS, pltpu.roll(top_x, DIRS, 2), top_y)
    gathered[j] = top.reshape(wx * wy, 2 * DIRS)
    copies = [
        copy(gathered.at[j], gathered.at[j], g_send.at[d], g_recv.at[d], (i, lax.rem(j + d, ny)))
        for d in range(1, ny)
    ]
    for c in copies:
        c.start()
    for c in range(3):
        new_e[c] = e[c]
        new_h[c] = h[c]
    stores = [
        pltpu.make_async_copy(new_e, out_e, store.at[0]),
        pltpu.make_async_copy(new_h, out_h, store.at[1]),
    ]
    for c in stores:
        c.start()
    for c in copies:
        c.wait()
    every = gathered[...].reshape(cells, 2 * DIRS)
    near, far = split(every)[:2]
    every = jnp.concatenate([near, near, far], 0)
    real = jnp.dot(table_c[...], every, preferred_element_type=jnp.float32)
    imag = jnp.dot(table_s[...], every, preferred_element_type=jnp.float32)
    for k in range(nx):
        partial[k, 0] = real[k * own:(k + 1) * own]
        partial[k, 1] = imag[k * own:(k + 1) * own]
    core = lax.rem(i, 2)
    mate = i + 1 - 2 * core
    chips = nx // 2
    order = list(range(1, chips)) + [0]
    pairs = {
        d: copy(
            partial.at[lax.rem(mate + 2 * d, nx)], paired.at[d], p_send.at[d], p_recv.at[d], (mate, j)
        )
        for d in order
    }
    for d in order:
        pairs[d].start()
    copies = []
    for d in order:
        mine = lax.rem(i + 2 * d, nx)
        pairs[d].wait_recv()
        if d:
            summed[d] = partial[mine] + paired[d]
            c = copy(summed.at[d], arrived.at[d], p_send.at[chips + d], p_recv.at[chips + d], (mine, j))
            c.start()
            copies.append(c)
    total = partial[i] + paired[0]
    for d, c in zip(order, copies):
        c.wait_recv()
        total = total + arrived[d]
    for c in copies + [pairs[d] for d in order]:
        c.wait_send()
    scale = 1.0 / math.sqrt(all_x * all_y)
    re, im = total[0] * scale, total[1] * -scale
    low = lanes_of(re.shape) < DIRS
    out_s[:, :2 * DIRS] = jnp.where(low, re, pltpu.roll(im, DIRS, 1))
    out_s[:, 2 * DIRS:] = jnp.where(low, pltpu.roll(re, DIRS, 1), im)
    for c in stores:
        c.wait()


def hand_over(from_e, from_h, from_s, to_e, to_h, to_s, via_e, via_h, via_s, sem):
    plan = ((from_e, via_e, to_e), (from_h, via_h, to_h), (from_s, via_s, to_s))
    loads = [pltpu.make_async_copy(src, via, sem.at[0, k]) for k, (src, via, _) in enumerate(plan)]
    stores = [pltpu.make_async_copy(via, dst, sem.at[1, k]) for k, (_, via, dst) in enumerate(plan)]
    for c in loads:
        c.start()
    for load, store in zip(loads, stores):
        load.wait()
        store.start()
    for c in stores:
        c.wait()


def local(nx, ny, te, th, fe, fh, classes, material, permittivity, contrast, orders):
    wx, wy = te.shape[1], te.shape[2]
    own = orders.shape[0] // (nx * ny)
    rows, cells = nx * own, ny * wx * wy
    f32 = jnp.float32
    vmem = pl.BlockSpec(memory_space=pltpu.VMEM)
    args = (
        te, th, jnp.transpose(fe, (0, 1, 3, 2)), jnp.transpose(fh, (0, 1, 3, 2)),
        jnp.transpose(classes, (0, 2, 1)), jnp.transpose(material, (0, 2, 1)),
        permittivity, contrast, jnp.transpose(orders),
    )

    def two(*shape):
        return [pltpu.VMEM((STEPS,) + shape, f32)] * 2

    hbm = pl.BlockSpec(memory_space=pltpu.HBM)
    out_shape = (
        jax.ShapeDtypeStruct(te.shape, f32),
        jax.ShapeDtypeStruct(th.shape, f32),
        jax.ShapeDtypeStruct((own, 4 * DIRS), f32),
    )
    results = pl.pallas_call(
        functools.partial(kernel, nx, ny, own),
        out_shape=out_shape,
        in_specs=[hbm] * 9,
        out_specs=(hbm, hbm, vmem),
        scratch_shapes=[
            *two(15, wy, HALF), *two(6, wy, HALF), *two(15, wx, HALF), *two(6, wx, HALF),
            *two(3, 1, HALF), *two(3, 1, HALF),
            pltpu.VMEM((ny, wx * wy, 2 * DIRS), f32),
            pltpu.VMEM((nx, 2, own, 2 * DIRS), f32),
            *[pltpu.VMEM((nx // 2, 2, own, 2 * DIRS), f32)] * 3,
            pltpu.VMEM((rows, 3 * cells), jnp.bfloat16),
            pltpu.VMEM((rows, 3 * cells), jnp.bfloat16),
            pltpu.SemaphoreType.DMA((6 * STEPS + 6,)), pltpu.SemaphoreType.DMA((6 * STEPS + 6,)),
            pltpu.SemaphoreType.DMA((ny,)), pltpu.SemaphoreType.DMA((ny,)),
            pltpu.SemaphoreType.DMA((nx,)), pltpu.SemaphoreType.DMA((nx,)),
            *[pltpu.VMEM(v.shape, v.dtype) for v in args[:6]],
            *[pltpu.SMEM(v.shape, v.dtype) for v in args[6:8]],
            pltpu.VMEM(args[8].shape, args[8].dtype),
            pltpu.SemaphoreType.DMA((9,)),
            pltpu.VMEM(te.shape, f32), pltpu.VMEM(th.shape, f32),
            pltpu.SemaphoreType.DMA((2,)),
        ],
        compiler_params=pltpu.CompilerParams(
            collective_id=0, has_side_effects=True, vmem_limit_bytes=64 * 1024 * 1024 - 65536
        ),
        name="slab",
    )(*args)
    return pl.pallas_call(
        hand_over,
        out_shape=out_shape,
        in_specs=[hbm] * 3,
        out_specs=(hbm, hbm, hbm),
        scratch_shapes=[pltpu.VMEM(v.shape, f32) for v in out_shape] + [pltpu.SemaphoreType.DMA((2, 3))],
        compiler_params=pltpu.CompilerParams(vmem_limit_bytes=64 * 1024 * 1024 - 65536),
        name="hand_over",
    )(*results)


def solution(mesh):
    in_specs = (
        P(None, "gx", "gy", None),
        P(None, "gx", "gy", None),
        P(None, "gx", "gy", None),
        P(None, "gx", "gy", None),
        P("gx", "gy", None),
        P("gx", "gy", None),
        P(),
        P(),
        P(),
    )
    out_specs = (P(None, "gx", "gy", None), P(None, "gx", "gy", None), P(("gx", "gy"), None))
    body = functools.partial(local, mesh.shape["gx"], mesh.shape["gy"])
    return jax.shard_map(body, mesh=mesh, in_specs=in_specs, out_specs=out_specs, check_vma=False)
```

```python
import functools
import math

import jax
import jax.numpy as jnp
from jax import lax
from jax.experimental import pallas as pl
from jax.experimental.pallas import tpu as pltpu
from jax.sharding import PartitionSpec as P

DIRS = 64
STEPS = 2
LAYERS = 4
WIDE = LAYERS * DIRS
HALF = WIDE // 2
time_step = 0.5


def lanes_of(shape):
    return lax.broadcasted_iota(jnp.int32, shape, len(shape) - 1)


def sublanes_of(shape):
    return lax.broadcasted_iota(jnp.int32, shape, len(shape) - 2)


def next_z(f):
    return jnp.where(lanes_of(f.shape) < WIDE - DIRS, pltpu.roll(f, WIDE - DIRS, f.ndim - 1), 0.0)


def prev_z(f):
    return jnp.where(lanes_of(f.shape) >= DIRS, pltpu.roll(f, DIRS, f.ndim - 1), 0.0)


def after_rows(f, row):
    n = f.shape[-2]
    return jnp.where(sublanes_of(f.shape) == n - 1, row, pltpu.roll(f, n - 1, f.ndim - 2))


def before_rows(f, row):
    return jnp.where(sublanes_of(f.shape) == 0, row, pltpu.roll(f, 1, f.ndim - 2))


def after_x(f, plane):
    return jnp.concatenate([f[1:], plane[None]], 0)


def before_x(f, plane):
    return jnp.concatenate([plane[None], f[:-1]], 0)


def packed(v):
    low, high = v[..., :HALF], v[..., HALF:]
    return jnp.where(lanes_of(low.shape) % DIRS < DIRS // 2, low, high)


def unpacked(v):
    near = lanes_of(v.shape) % DIRS < DIRS // 2
    axis = v.ndim - 1
    low = jnp.where(near, v, pltpu.roll(v, DIRS // 2, axis))
    high = jnp.where(near, pltpu.roll(v, HALF - DIRS // 2, axis), v)
    return jnp.concatenate([low, high], axis)


def take(buf, at, n):
    tangent = [jnp.concatenate([buf[at, 2 * k], buf[at, 2 * k + 1]], -1) for k in range(n)]
    forward = [unpacked(buf[at, 2 * n + k]) for k in range(n)]
    return (tangent, forward)


def sine(turn):
    u = turn * (2.0 * math.pi)
    s = u * u
    poly = -1.0 / 39916800.0
    for c in (1.0 / 362880.0, -1.0 / 5040.0, 1.0 / 120.0, -1.0 / 6.0):
        poly = poly * s + c
    return u + u * (s * poly)


def half_step_h(e, h, rim):
    ex, ey, ez = e
    hx, hy, hz = h
    xp, yp, xm, ym, cx, cy = rim
    new = (
        hx - time_step * ((after_rows(ez, yp[1][:, None, :]) - ez) - (next_z(ey) - ey)),
        hy - time_step * ((next_z(ex) - ex) - (after_x(ez, xp[1]) - ez)),
        hz - time_step * ((after_x(ey, xp[0]) - ey) - (after_rows(ex, yp[0][:, None, :]) - ex)),
    )
    x_y = xm[3] - time_step * ((next_z(xm[0]) - xm[0]) - (ez[0] - xm[2]))
    x_z = xm[4] - time_step * ((ey[0] - xm[1]) - (after_rows(xm[0], cx) - xm[0]))
    y_x = ym[3] - time_step * ((ez[:, 0, :] - ym[2]) - (next_z(ym[1]) - ym[1]))
    y_z = ym[4] - time_step * ((after_rows(ym[1], cy) - ym[1]) - (ex[:, 0, :] - ym[0]))
    return new, (x_y, x_z, y_x, y_z)


def curl_b(h, rim):
    hx, hy, hz = h
    x_y, x_z, y_x, y_z = rim
    return (
        (hz - before_rows(hz, y_z[:, None, :])) - (hy - prev_z(hy)),
        (hx - prev_z(hx)) - (hz - before_x(hz, x_z)),
        (hy - before_x(hy, x_y)) - (hx - before_rows(hx, y_x[:, None, :])),
    )


def split(v):
    parts = []
    for _ in range(3):
        parts.append(v.astype(jnp.bfloat16))
        v = v - parts[-1].astype(jnp.float32)
    return parts


def widened(layers, ny):
    lead = layers[0].shape[0]
    flat = LAYERS * ny
    total = 0.0
    for z in range(LAYERS):
        for k, part in enumerate(split(layers[z])):
            place = (
                lax.broadcasted_iota(jnp.int32, (ny, 3 * flat), 1)
                == lax.broadcasted_iota(jnp.int32, (ny, 3 * flat), 0) + (k * flat + z * ny)
            ).astype(jnp.float32)
            total = total + jnp.dot(part, place.astype(jnp.bfloat16), preferred_element_type=jnp.float32)
    rows = jnp.broadcast_to(total[:, None, :], (lead, ny, 3 * flat))
    rows = jnp.where(lanes_of(rows.shape) % ny == sublanes_of(rows.shape), rows, 0.0)
    spread = (
        (lax.broadcasted_iota(jnp.int32, (3 * flat, WIDE), 0) // ny) % LAYERS
        == lax.broadcasted_iota(jnp.int32, (3 * flat, WIDE), 1) // DIRS
    ).astype(jnp.float32)
    wide = jnp.dot(
        rows.reshape(lead * ny, 3 * flat).astype(jnp.bfloat16),
        spread.astype(jnp.bfloat16),
        preferred_element_type=jnp.float32,
    )
    return wide.reshape(lead, ny, WIDE)


def kernel(
    nx, ny, own,
    te_at, th_at, fe_at, fh_at, classes_at, material_at, permittivity_at, contrast_at, orders_at,
    out_e, out_h, out_s,
    s_xm, r_xm, s_xp, r_xp, s_ym, r_ym, s_yp, r_yp, s_cx, r_cx, s_cy, r_cy,
    gathered, partial, paired, summed, arrived, table,
    rim_send, rim_recv, g_send, g_recv, p_send, p_recv,
    te, th, fe, fh, classes, material, permittivity, contrast, orders, load, new_e, new_h, store,
):
    loads = [
        pltpu.make_async_copy(src, dst, load.at[k])
        for k, (src, dst) in enumerate((
            *[(src.at[c], dst.at[c]) for c in range(3) for src, dst in ((te_at, te), (th_at, th))],
            (fe_at, fe), (fh_at, fh), (classes_at, classes),
            (material_at, material), (permittivity_at, permittivity), (contrast_at, contrast),
            (orders_at, orders),
        ))
    ]
    for c in loads:
        c.start()
    wx, wy = te.shape[1], te.shape[2]
    i, j = lax.axis_index("gx"), lax.axis_index("gy")
    up, down = lax.rem(i + 1, nx), lax.rem(i + nx - 1, nx)
    right, left = lax.rem(j + 1, ny), lax.rem(j + ny - 1, ny)
    barrier = pltpu.get_barrier_semaphore()
    offsets = sorted({1, nx - 1, *range(2, nx, 2)})
    peers = [(lax.rem(i + d, nx), j) for d in offsets]
    peers += [(i, lax.rem(j + d, ny)) for d in range(1, ny)]
    peers += [(up, left), (down, right)]
    for peer in peers:
        pl.semaphore_signal(barrier, inc=1, device_id=peer, device_id_type=pl.DeviceIdType.MESH)

    def copy(src, dst, send, recv, device):
        return pltpu.make_async_remote_copy(
            src_ref=src, dst_ref=dst, send_sem=send, recv_sem=recv,
            device_id=device, device_id_type=pl.DeviceIdType.MESH,
        )

    def planes_of(e, h):
        return (
            [f[:, wy - 1, :] for f in (e[0], e[1], e[2], h[0], h[2])],
            [f[wx - 1] for f in (e[0], e[1], e[2], h[1], h[2])],
            [e[0][:, 0, :], e[2][:, 0, :]],
            [e[1][0], e[2][0]],
            [e[0][wx - 1, 0:1, :]],
            [e[1][0, wy - 1:wy, :]],
        )

    rims = (
        (s_ym, r_ym, (i, right)), (s_xm, r_xm, (up, j)), (s_yp, r_yp, (i, left)),
        (s_xp, r_xp, (down, j)), (s_cx, r_cx, (up, left)), (s_cy, r_cy, (down, right)),
    )

    def put_tangent(step, e, h):
        for (buf, _, _), planes in zip(rims, planes_of(e, h)):
            for k, plane in enumerate(planes):
                buf[step, 2 * k] = plane[:, :HALF]
                buf[step, 2 * k + 1] = plane[:, HALF:]

    def put_forward(step, e, h):
        for (buf, _, _), planes in zip(rims, planes_of(e, h)):
            for k, plane in enumerate(planes):
                buf[step, 2 * len(planes) + k] = packed(plane)

    def send(step, first, part):
        copies = []
        for k, (s, r, device) in enumerate(rims):
            n = s.shape[1] // 3
            span = (pl.ds(0, 3 * n), pl.ds(0, 2 * n), pl.ds(2 * n, n))[part]
            copies.append(copy(
                s.at[step, span], r.at[step, span], rim_send.at[first + k], rim_recv.at[first + k], device
            ))
        for c in copies:
            c.start()
        return copies

    for c in loads[:6]:
        c.wait()
    e = [te[c] for c in range(3)]
    h = [th[c] for c in range(3)]
    put_tangent(0, e, h)
    pl.semaphore_wait(barrier, len(peers))
    waiting = send(0, 0, 1)
    for c in loads[6:]:
        c.wait()
    layers = []
    for z in range(LAYERS):
        layers.append(jnp.concatenate([
            fe[:, :, z, :].reshape(3 * wx, wy), fh[:, :, z, :].reshape(3 * wx, wy),
            classes[:, z, :].astype(jnp.float32), material[:, z, :].astype(jnp.float32),
        ], 0))
    wide = widened(layers, wy)
    fwd_e = [wide[c * wx:(c + 1) * wx] for c in range(3)]
    fwd_h = [wide[c * wx:(c + 1) * wx] for c in range(3, 6)]
    put_forward(0, fwd_e, fwd_h)
    waiting += send(0, 6, 2)

    kind = wide[7 * wx:]
    eps = jnp.zeros_like(kind)
    slope = jnp.zeros_like(kind)
    for k in range(permittivity.shape[0]):
        eps = jnp.where(kind == float(k), permittivity[k], eps)
        slope = jnp.where(kind == float(k), contrast[k], slope)
    inverse = time_step / eps
    coef = time_step * slope / (eps * eps)
    hot = wide[6 * wx:7 * wx] == (lanes_of(kind.shape) % DIRS).astype(jnp.float32)
    coef = jnp.where(hot, coef, 0.0)

    rows, cells = nx * own, ny * wx * wy
    count = orders.shape[1]
    row = lax.broadcasted_iota(jnp.int32, (rows, 1), 0)
    target = (row // own) * (ny * own) + j * own + row % own
    pick = (lax.broadcasted_iota(jnp.int32, (rows, count), 1) == target).astype(jnp.float32)
    pair = lax.dot_general(
        pick.astype(jnp.bfloat16), orders[...].astype(jnp.float32).astype(jnp.bfloat16),
        (((1,), (1,)), ((), ())), preferred_element_type=jnp.float32,
    )
    cell = lax.broadcasted_iota(jnp.int32, (1, cells), 1)
    all_x, all_y = nx * wx, ny * wy
    x_at = ((i * wx + (cell // wy) % wx) * all_y).astype(jnp.float32)
    y_at = (((cell // (wx * wy)) * wy + cell % wy) * all_x).astype(jnp.float32)
    index = pair[:, 0:1] * x_at + pair[:, 1:2] * y_at
    index = index - float(all_x * all_y) * jnp.round(index * (1.0 / (all_x * all_y)))
    turn = index * (1.0 / (all_x * all_y))
    cosine = sine(0.25 - jnp.abs(turn))
    sines = sine(jnp.where(turn > 0.25, 0.5 - turn, jnp.where(turn < -0.25, -0.5 - turn, turn)))
    block = wx * wy
    for at, value in ((0, cosine), (rows, sines)):
        near, far = split(value)[:2]
        for k in range(ny):
            for q, part in enumerate((near, far, near)):
                table[k, at:at + rows, q * block:(q + 1) * block] = part[:, k * block:(k + 1) * block]

    for step in range(STEPS):
        for c in waiting:
            c.wait()
        xm, ym = take(r_xm, step, 5), take(r_ym, step, 5)
        xp, yp = take(r_xp, step, 2), take(r_yp, step, 2)
        cx, cy = take(r_cx, step, 1), take(r_cy, step, 1)
        fwd_h, rim = half_step_h(fwd_e, fwd_h, (xp[1], yp[1], xm[1], ym[1], cx[1][0], cy[1][0]))
        fwd_c = curl_b(fwd_h, rim)
        fwd_e = [fwd_e[c] + inverse * fwd_c[c] for c in range(3)]
        h, rim = half_step_h(e, h, (xp[0], yp[0], xm[0], ym[0], cx[0][0], cy[0][0]))
        tan_c = curl_b(h, rim)
        e = [e[c] + inverse * tan_c[c] - coef * fwd_c[c] for c in range(3)]
        if step < STEPS - 1:
            put_tangent(step + 1, e, h)
            put_forward(step + 1, fwd_e, fwd_h)
            waiting = send(step + 1, 12 + 6 * step, 0)

    top_x, top_y = e[0][:, :, HALF:], e[1][:, :, HALF:]
    top = jnp.where(lanes_of(top_x.shape) < DIRS, pltpu.roll(top_x, DIRS, 2), top_y)
    gathered[j] = top.reshape(wx * wy, 2 * DIRS)
    copies = [
        copy(gathered.at[j], gathered.at[j], g_send.at[d], g_recv.at[d], (i, lax.rem(j + d, ny)))
        for d in range(1, ny)
    ]
    for c in copies:
        c.start()
    for c in range(3):
        new_e[c] = e[c]
        new_h[c] = h[c]
    stores = [
        pltpu.make_async_copy(new_e, out_e, store.at[0]),
        pltpu.make_async_copy(new_h, out_h, store.at[1]),
    ]
    for c in stores:
        c.start()
    def product(source):
        near, far = split(gathered[source])[:2]
        return jnp.dot(
            table[source], jnp.concatenate([near, near, far], 0), preferred_element_type=jnp.float32
        )

    sums = product(j)
    for d, c in zip(range(1, ny), copies):
        c.wait_recv()
        sums = sums + product(lax.rem(j + ny - d, ny))
    for c in copies:
        c.wait_send()
    for k in range(nx):
        partial[k, 0] = sums[k * own:(k + 1) * own]
        partial[k, 1] = sums[rows + k * own:rows + (k + 1) * own]
    core = lax.rem(i, 2)
    mate = i + 1 - 2 * core
    chips = nx // 2
    order = list(range(1, chips)) + [0]
    pairs = {
        d: copy(
            partial.at[lax.rem(mate + 2 * d, nx)], paired.at[d], p_send.at[d], p_recv.at[d], (mate, j)
        )
        for d in order
    }
    for d in order:
        pairs[d].start()
    copies = []
    for d in order:
        mine = lax.rem(i + 2 * d, nx)
        pairs[d].wait_recv()
        if d:
            summed[d] = partial[mine] + paired[d]
            c = copy(summed.at[d], arrived.at[d], p_send.at[chips + d], p_recv.at[chips + d], (mine, j))
            c.start()
            copies.append(c)
    total = partial[i] + paired[0]
    for d, c in zip(order, copies):
        c.wait_recv()
        total = total + arrived[d]
    for c in copies + [pairs[d] for d in order]:
        c.wait_send()
    scale = 1.0 / math.sqrt(all_x * all_y)
    re, im = total[0] * scale, total[1] * -scale
    low = lanes_of(re.shape) < DIRS
    out_s[:, :2 * DIRS] = jnp.where(low, re, pltpu.roll(im, DIRS, 1))
    out_s[:, 2 * DIRS:] = jnp.where(low, pltpu.roll(re, DIRS, 1), im)
    for c in stores:
        c.wait()


def hand_over(from_e, from_h, from_s, to_e, to_h, to_s, via_e, via_h, via_s, sem):
    plan = [
        (src.at[c], via.at[c], dst.at[c])
        for c in range(3) for src, via, dst in ((from_e, via_e, to_e), (from_h, via_h, to_h))
    ]
    plan.append((from_s, via_s, to_s))
    loads = [pltpu.make_async_copy(src, via, sem.at[0, k]) for k, (src, via, _) in enumerate(plan)]
    stores = [pltpu.make_async_copy(via, dst, sem.at[1, k]) for k, (_, via, dst) in enumerate(plan)]
    for c in loads:
        c.start()
    for load, store in zip(loads, stores):
        load.wait()
        store.start()
    for c in stores:
        c.wait()


def local(nx, ny, te, th, fe, fh, classes, material, permittivity, contrast, orders):
    wx, wy = te.shape[1], te.shape[2]
    own = orders.shape[0] // (nx * ny)
    rows = nx * own
    f32 = jnp.float32
    vmem = pl.BlockSpec(memory_space=pltpu.VMEM)
    args = (
        te, th, jnp.transpose(fe, (0, 1, 3, 2)), jnp.transpose(fh, (0, 1, 3, 2)),
        jnp.transpose(classes, (0, 2, 1)), jnp.transpose(material, (0, 2, 1)),
        permittivity, contrast, jnp.transpose(orders),
    )

    def two(*shape):
        return [pltpu.VMEM((STEPS,) + shape, f32)] * 2

    hbm = pl.BlockSpec(memory_space=pltpu.HBM)
    out_shape = (
        jax.ShapeDtypeStruct(te.shape, f32),
        jax.ShapeDtypeStruct(th.shape, f32),
        jax.ShapeDtypeStruct((own, 4 * DIRS), f32),
    )
    results = pl.pallas_call(
        functools.partial(kernel, nx, ny, own),
        out_shape=out_shape,
        in_specs=[hbm] * 9,
        out_specs=(hbm, hbm, vmem),
        scratch_shapes=[
            *two(15, wy, HALF), *two(6, wy, HALF), *two(15, wx, HALF), *two(6, wx, HALF),
            *two(3, 1, HALF), *two(3, 1, HALF),
            pltpu.VMEM((ny, wx * wy, 2 * DIRS), f32),
            pltpu.VMEM((nx, 2, own, 2 * DIRS), f32),
            *[pltpu.VMEM((nx // 2, 2, own, 2 * DIRS), f32)] * 3,
            pltpu.VMEM((ny, 2 * rows, 3 * wx * wy), jnp.bfloat16),
            pltpu.SemaphoreType.DMA((6 * STEPS + 6,)), pltpu.SemaphoreType.DMA((6 * STEPS + 6,)),
            pltpu.SemaphoreType.DMA((ny,)), pltpu.SemaphoreType.DMA((ny,)),
            pltpu.SemaphoreType.DMA((nx,)), pltpu.SemaphoreType.DMA((nx,)),
            *[pltpu.VMEM(v.shape, v.dtype) for v in args[:6]],
            *[pltpu.SMEM(v.shape, v.dtype) for v in args[6:8]],
            pltpu.VMEM(args[8].shape, args[8].dtype),
            pltpu.SemaphoreType.DMA((13,)),
            pltpu.VMEM(te.shape, f32), pltpu.VMEM(th.shape, f32),
            pltpu.SemaphoreType.DMA((2,)),
        ],
        compiler_params=pltpu.CompilerParams(
            collective_id=0, has_side_effects=True, vmem_limit_bytes=64 * 1024 * 1024 - 65536
        ),
        name="slab",
    )(*args)
    return pl.pallas_call(
        hand_over,
        out_shape=out_shape,
        in_specs=[hbm] * 3,
        out_specs=(hbm, hbm, hbm),
        scratch_shapes=[pltpu.VMEM(v.shape, f32) for v in out_shape] + [pltpu.SemaphoreType.DMA((2, 7))],
        compiler_params=pltpu.CompilerParams(vmem_limit_bytes=64 * 1024 * 1024 - 65536),
        name="hand_over",
    )(*results)


def solution(mesh):
    in_specs = (
        P(None, "gx", "gy", None),
        P(None, "gx", "gy", None),
        P(None, "gx", "gy", None),
        P(None, "gx", "gy", None),
        P("gx", "gy", None),
        P("gx", "gy", None),
        P(),
        P(),
        P(),
    )
    out_specs = (P(None, "gx", "gy", None), P(None, "gx", "gy", None), P(("gx", "gy"), None))
    body = functools.partial(local, mesh.shape["gx"], mesh.shape["gy"])
    return jax.shard_map(body, mesh=mesh, in_specs=in_specs, out_specs=out_specs, check_vma=False)
```

```python
import functools
import math

import jax
import jax.numpy as jnp
from jax import lax
from jax.experimental import pallas as pl
from jax.experimental.pallas import tpu as pltpu
from jax.sharding import PartitionSpec as P

DIRS = 64
STEPS = 2
LAYERS = 4
WIDE = LAYERS * DIRS
HALF = WIDE // 2
time_step = 0.5


def lanes_of(shape):
    return lax.broadcasted_iota(jnp.int32, shape, len(shape) - 1)


def sublanes_of(shape):
    return lax.broadcasted_iota(jnp.int32, shape, len(shape) - 2)


def next_z(f):
    return jnp.where(lanes_of(f.shape) < WIDE - DIRS, pltpu.roll(f, WIDE - DIRS, f.ndim - 1), 0.0)


def prev_z(f):
    return jnp.where(lanes_of(f.shape) >= DIRS, pltpu.roll(f, DIRS, f.ndim - 1), 0.0)


def after_rows(f, row):
    n = f.shape[-2]
    return jnp.where(sublanes_of(f.shape) == n - 1, row, pltpu.roll(f, n - 1, f.ndim - 2))


def before_rows(f, row):
    return jnp.where(sublanes_of(f.shape) == 0, row, pltpu.roll(f, 1, f.ndim - 2))


def after_x(f, plane):
    return jnp.concatenate([f[1:], plane[None]], 0)


def before_x(f, plane):
    return jnp.concatenate([plane[None], f[:-1]], 0)


def packed(v):
    low, high = v[..., :HALF], v[..., HALF:]
    return jnp.where(lanes_of(low.shape) % DIRS < DIRS // 2, low, high)


def unpacked(v):
    near = lanes_of(v.shape) % DIRS < DIRS // 2
    axis = v.ndim - 1
    low = jnp.where(near, v, pltpu.roll(v, DIRS // 2, axis))
    high = jnp.where(near, pltpu.roll(v, HALF - DIRS // 2, axis), v)
    return jnp.concatenate([low, high], axis)


SHARE = 4
PIECE = DIRS // 2 // SHARE


def dense(planes):
    values = [packed(p) for p in planes]
    place = lanes_of(values[0].shape) % (DIRS // 2) // PIECE
    result = values[0]
    for q in range(1, len(values)):
        result = jnp.where(place == q, values[q], result)
    return result


def plane_of(v, q):
    place = lanes_of(v.shape) % (DIRS // 2) // PIECE
    result = v
    for r in range(SHARE):
        if r != q:
            result = jnp.where(place == r, pltpu.roll(v, (PIECE * (r - q)) % HALF, v.ndim - 1), result)
    return unpacked(result)


def take(buf, at, n):
    tangent = [jnp.concatenate([buf[at, 2 * k], buf[at, 2 * k + 1]], -1) for k in range(n)]
    forward = [plane_of(buf[at, 2 * n + k // SHARE], k % SHARE) for k in range(n)]
    return (tangent, forward)


def sine(turn):
    u = turn * (2.0 * math.pi)
    s = u * u
    poly = -1.0 / 39916800.0
    for c in (1.0 / 362880.0, -1.0 / 5040.0, 1.0 / 120.0, -1.0 / 6.0):
        poly = poly * s + c
    return u + u * (s * poly)


def half_step_h(e, h, rim):
    ex, ey, ez = e
    hx, hy, hz = h
    xp, yp, xm, ym, cx, cy = rim
    new = (
        hx - time_step * ((after_rows(ez, yp[1][:, None, :]) - ez) - (next_z(ey) - ey)),
        hy - time_step * ((next_z(ex) - ex) - (after_x(ez, xp[1]) - ez)),
        hz - time_step * ((after_x(ey, xp[0]) - ey) - (after_rows(ex, yp[0][:, None, :]) - ex)),
    )
    x_y = xm[3] - time_step * ((next_z(xm[0]) - xm[0]) - (ez[0] - xm[2]))
    x_z = xm[4] - time_step * ((ey[0] - xm[1]) - (after_rows(xm[0], cx) - xm[0]))
    y_x = ym[3] - time_step * ((ez[:, 0, :] - ym[2]) - (next_z(ym[1]) - ym[1]))
    y_z = ym[4] - time_step * ((after_rows(ym[1], cy) - ym[1]) - (ex[:, 0, :] - ym[0]))
    return new, (x_y, x_z, y_x, y_z)


def curl_b(h, rim):
    hx, hy, hz = h
    x_y, x_z, y_x, y_z = rim
    return (
        (hz - before_rows(hz, y_z[:, None, :])) - (hy - prev_z(hy)),
        (hx - prev_z(hx)) - (hz - before_x(hz, x_z)),
        (hy - before_x(hy, x_y)) - (hx - before_rows(hx, y_x[:, None, :])),
    )


def split(v):
    parts = []
    for _ in range(3):
        parts.append(v.astype(jnp.bfloat16))
        v = v - parts[-1].astype(jnp.float32)
    return parts


def widened(layers, ny):
    lead = layers[0].shape[0]
    flat = LAYERS * ny
    total = 0.0
    for z in range(LAYERS):
        for k, part in enumerate(split(layers[z])):
            place = (
                lax.broadcasted_iota(jnp.int32, (ny, 3 * flat), 1)
                == lax.broadcasted_iota(jnp.int32, (ny, 3 * flat), 0) + (k * flat + z * ny)
            ).astype(jnp.float32)
            total = total + jnp.dot(part, place.astype(jnp.bfloat16), preferred_element_type=jnp.float32)
    rows = jnp.broadcast_to(total[:, None, :], (lead, ny, 3 * flat))
    rows = jnp.where(lanes_of(rows.shape) % ny == sublanes_of(rows.shape), rows, 0.0)
    spread = (
        (lax.broadcasted_iota(jnp.int32, (3 * flat, WIDE), 0) // ny) % LAYERS
        == lax.broadcasted_iota(jnp.int32, (3 * flat, WIDE), 1) // DIRS
    ).astype(jnp.float32)
    wide = jnp.dot(
        rows.reshape(lead * ny, 3 * flat).astype(jnp.bfloat16),
        spread.astype(jnp.bfloat16),
        preferred_element_type=jnp.float32,
    )
    return wide.reshape(lead, ny, WIDE)


def kernel(
    nx, ny, own,
    te_at, th_at, fe_at, fh_at, classes_at, material_at, permittivity_at, contrast_at, orders_at,
    out_e, out_h, out_s,
    s_xm, r_xm, s_xp, r_xp, s_ym, r_ym, s_yp, r_yp, s_cx, r_cx, s_cy, r_cy,
    gathered, partial, paired, summed, arrived, table,
    rim_send, rim_recv, g_send, g_recv, p_send, p_recv,
    te, th, fe, fh, classes, material, permittivity, contrast, orders, load, new_e, new_h, store,
):
    loads = [
        pltpu.make_async_copy(src, dst, load.at[k])
        for k, (src, dst) in enumerate((
            *[(src.at[c], dst.at[c]) for c in range(3) for src, dst in ((te_at, te), (th_at, th))],
            (fe_at, fe), (fh_at, fh), (classes_at, classes),
            (material_at, material), (permittivity_at, permittivity), (contrast_at, contrast),
            (orders_at, orders),
        ))
    ]
    for c in loads:
        c.start()
    wx, wy = te.shape[1], te.shape[2]
    i, j = lax.axis_index("gx"), lax.axis_index("gy")
    up, down = lax.rem(i + 1, nx), lax.rem(i + nx - 1, nx)
    right, left = lax.rem(j + 1, ny), lax.rem(j + ny - 1, ny)
    barrier = pltpu.get_barrier_semaphore()
    offsets = sorted({1, nx - 1, *range(2, nx, 2)})
    peers = [(lax.rem(i + d, nx), j) for d in offsets]
    peers += [(i, lax.rem(j + d, ny)) for d in range(1, ny)]
    peers += [(up, left), (down, right)]
    for peer in peers:
        pl.semaphore_signal(barrier, inc=1, device_id=peer, device_id_type=pl.DeviceIdType.MESH)

    def copy(src, dst, send, recv, device):
        return pltpu.make_async_remote_copy(
            src_ref=src, dst_ref=dst, send_sem=send, recv_sem=recv,
            device_id=device, device_id_type=pl.DeviceIdType.MESH,
        )

    def planes_of(e, h):
        return (
            [f[:, wy - 1, :] for f in (e[0], e[1], e[2], h[0], h[2])],
            [f[wx - 1] for f in (e[0], e[1], e[2], h[1], h[2])],
            [e[0][:, 0, :], e[2][:, 0, :]],
            [e[1][0], e[2][0]],
            [e[0][wx - 1, 0:1, :]],
            [e[1][0, wy - 1:wy, :]],
        )

    rims = (
        (s_ym, r_ym, (i, right)), (s_xm, r_xm, (up, j)), (s_yp, r_yp, (i, left)),
        (s_xp, r_xp, (down, j)), (s_cx, r_cx, (up, left)), (s_cy, r_cy, (down, right)),
    )

    def put_tangent(step, e, h):
        for (buf, _, _), planes in zip(rims, planes_of(e, h)):
            for k, plane in enumerate(planes):
                buf[step, 2 * k] = plane[:, :HALF]
                buf[step, 2 * k + 1] = plane[:, HALF:]

    def put_forward(step, e, h):
        for (buf, _, _), planes in zip(rims, planes_of(e, h)):
            n = len(planes)
            for k in range(0, n, SHARE):
                buf[step, 2 * n + k // SHARE] = dense(planes[k:k + SHARE])

    def send(step, first, part):
        copies = []
        for k, (s, r, device) in enumerate(rims):
            n = (5, 5, 2, 2, 1, 1)[k]
            extra = s.shape[1] - 2 * n
            span = (pl.ds(0, 2 * n + extra), pl.ds(0, 2 * n), pl.ds(2 * n, extra))[part]
            copies.append(copy(
                s.at[step, span], r.at[step, span], rim_send.at[first + k], rim_recv.at[first + k], device
            ))
        for c in copies:
            c.start()
        return copies

    for c in loads[:6]:
        c.wait()
    e = [te[c] for c in range(3)]
    h = [th[c] for c in range(3)]
    put_tangent(0, e, h)
    pl.semaphore_wait(barrier, len(peers))
    waiting = send(0, 0, 1)
    for c in loads[6:]:
        c.wait()
    layers = []
    for z in range(LAYERS):
        layers.append(jnp.concatenate([
            fe[:, :, z, :].reshape(3 * wx, wy), fh[:, :, z, :].reshape(3 * wx, wy),
            classes[:, z, :].astype(jnp.float32), material[:, z, :].astype(jnp.float32),
        ], 0))
    wide = widened(layers, wy)
    fwd_e = [wide[c * wx:(c + 1) * wx] for c in range(3)]
    fwd_h = [wide[c * wx:(c + 1) * wx] for c in range(3, 6)]
    put_forward(0, fwd_e, fwd_h)
    waiting += send(0, 6, 2)

    kind = wide[7 * wx:]
    eps = jnp.zeros_like(kind)
    slope = jnp.zeros_like(kind)
    for k in range(permittivity.shape[0]):
        eps = jnp.where(kind == float(k), permittivity[k], eps)
        slope = jnp.where(kind == float(k), contrast[k], slope)
    inverse = time_step / eps
    coef = time_step * slope / (eps * eps)
    hot = wide[6 * wx:7 * wx] == (lanes_of(kind.shape) % DIRS).astype(jnp.float32)
    coef = jnp.where(hot, coef, 0.0)

    rows, cells = nx * own, ny * wx * wy
    count = orders.shape[1]
    row = lax.broadcasted_iota(jnp.int32, (rows, 1), 0)
    target = (row // own) * (ny * own) + j * own + row % own
    pick = (lax.broadcasted_iota(jnp.int32, (rows, count), 1) == target).astype(jnp.float32)
    pair = lax.dot_general(
        pick.astype(jnp.bfloat16), orders[...].astype(jnp.float32).astype(jnp.bfloat16),
        (((1,), (1,)), ((), ())), preferred_element_type=jnp.float32,
    )
    cell = lax.broadcasted_iota(jnp.int32, (1, cells), 1)
    all_x, all_y = nx * wx, ny * wy
    x_at = ((i * wx + (cell // wy) % wx) * all_y).astype(jnp.float32)
    y_at = (((cell // (wx * wy)) * wy + cell % wy) * all_x).astype(jnp.float32)
    index = pair[:, 0:1] * x_at + pair[:, 1:2] * y_at
    index = index - float(all_x * all_y) * jnp.round(index * (1.0 / (all_x * all_y)))
    turn = index * (1.0 / (all_x * all_y))
    cosine = sine(0.25 - jnp.abs(turn))
    sines = sine(jnp.where(turn > 0.25, 0.5 - turn, jnp.where(turn < -0.25, -0.5 - turn, turn)))
    block = wx * wy
    for at, value in ((0, cosine), (rows, sines)):
        near, far = split(value)[:2]
        for k in range(ny):
            for q, part in enumerate((near, far, near)):
                table[k, at:at + rows, q * block:(q + 1) * block] = part[:, k * block:(k + 1) * block]

    for step in range(STEPS):
        for c in waiting:
            c.wait()
        xm, ym = take(r_xm, step, 5), take(r_ym, step, 5)
        xp, yp = take(r_xp, step, 2), take(r_yp, step, 2)
        cx, cy = take(r_cx, step, 1), take(r_cy, step, 1)
        fwd_h, rim = half_step_h(fwd_e, fwd_h, (xp[1], yp[1], xm[1], ym[1], cx[1][0], cy[1][0]))
        fwd_c = curl_b(fwd_h, rim)
        fwd_e = [fwd_e[c] + inverse * fwd_c[c] for c in range(3)]
        h, rim = half_step_h(e, h, (xp[0], yp[0], xm[0], ym[0], cx[0][0], cy[0][0]))
        tan_c = curl_b(h, rim)
        e = [e[c] + inverse * tan_c[c] - coef * fwd_c[c] for c in range(3)]
        if step < STEPS - 1:
            put_tangent(step + 1, e, h)
            put_forward(step + 1, fwd_e, fwd_h)
            waiting = send(step + 1, 12 + 6 * step, 0)

    top_x, top_y = e[0][:, :, HALF:], e[1][:, :, HALF:]
    top = jnp.where(lanes_of(top_x.shape) < DIRS, pltpu.roll(top_x, DIRS, 2), top_y)
    gathered[j] = top.reshape(wx * wy, 2 * DIRS)
    copies = [
        copy(gathered.at[j], gathered.at[j], g_send.at[d], g_recv.at[d], (i, lax.rem(j + d, ny)))
        for d in range(1, ny)
    ]
    for c in copies:
        c.start()
    for c in range(3):
        new_e[c] = e[c]
        new_h[c] = h[c]
    stores = [
        pltpu.make_async_copy(new_e, out_e, store.at[0]),
        pltpu.make_async_copy(new_h, out_h, store.at[1]),
    ]
    for c in stores:
        c.start()
    def product(source):
        near, far = split(gathered[source])[:2]
        return jnp.dot(
            table[source], jnp.concatenate([near, near, far], 0), preferred_element_type=jnp.float32
        )

    sums = product(j)
    for d, c in zip(range(1, ny), copies):
        c.wait_recv()
        sums = sums + product(lax.rem(j + ny - d, ny))
    for c in copies:
        c.wait_send()
    for k in range(nx):
        partial[k, 0] = sums[k * own:(k + 1) * own]
        partial[k, 1] = sums[rows + k * own:rows + (k + 1) * own]
    core = lax.rem(i, 2)
    mate = i + 1 - 2 * core
    chips = nx // 2
    order = list(range(1, chips)) + [0]
    pairs = {
        d: copy(
            partial.at[lax.rem(mate + 2 * d, nx)], paired.at[d], p_send.at[d], p_recv.at[d], (mate, j)
        )
        for d in order
    }
    for d in order:
        pairs[d].start()
    copies = []
    for d in order:
        mine = lax.rem(i + 2 * d, nx)
        pairs[d].wait_recv()
        if d:
            summed[d] = partial[mine] + paired[d]
            c = copy(summed.at[d], arrived.at[d], p_send.at[chips + d], p_recv.at[chips + d], (mine, j))
            c.start()
            copies.append(c)
    total = partial[i] + paired[0]
    for d, c in zip(order, copies):
        c.wait_recv()
        total = total + arrived[d]
    for c in copies + [pairs[d] for d in order]:
        c.wait_send()
    scale = 1.0 / math.sqrt(all_x * all_y)
    re, im = total[0] * scale, total[1] * -scale
    low = lanes_of(re.shape) < DIRS
    out_s[:, :2 * DIRS] = jnp.where(low, re, pltpu.roll(im, DIRS, 1))
    out_s[:, 2 * DIRS:] = jnp.where(low, pltpu.roll(re, DIRS, 1), im)
    for c in stores:
        c.wait()


def hand_over(from_e, from_h, from_s, to_e, to_h, to_s, via_e, via_h, via_s, sem):
    plan = [
        (src.at[c], via.at[c], dst.at[c])
        for c in range(3) for src, via, dst in ((from_e, via_e, to_e), (from_h, via_h, to_h))
    ]
    plan.append((from_s, via_s, to_s))
    loads = [pltpu.make_async_copy(src, via, sem.at[0, k]) for k, (src, via, _) in enumerate(plan)]
    stores = [pltpu.make_async_copy(via, dst, sem.at[1, k]) for k, (_, via, dst) in enumerate(plan)]
    for c in loads:
        c.start()
    for load, store in zip(loads, stores):
        load.wait()
        store.start()
    for c in stores:
        c.wait()


def local(nx, ny, te, th, fe, fh, classes, material, permittivity, contrast, orders):
    wx, wy = te.shape[1], te.shape[2]
    own = orders.shape[0] // (nx * ny)
    rows = nx * own
    f32 = jnp.float32
    vmem = pl.BlockSpec(memory_space=pltpu.VMEM)
    args = (
        te, th, jnp.transpose(fe, (0, 1, 3, 2)), jnp.transpose(fh, (0, 1, 3, 2)),
        jnp.transpose(classes, (0, 2, 1)), jnp.transpose(material, (0, 2, 1)),
        permittivity, contrast, jnp.transpose(orders),
    )

    def two(*shape):
        return [pltpu.VMEM((STEPS,) + shape, f32)] * 2

    hbm = pl.BlockSpec(memory_space=pltpu.HBM)
    out_shape = (
        jax.ShapeDtypeStruct(te.shape, f32),
        jax.ShapeDtypeStruct(th.shape, f32),
        jax.ShapeDtypeStruct((own, 4 * DIRS), f32),
    )
    results = pl.pallas_call(
        functools.partial(kernel, nx, ny, own),
        out_shape=out_shape,
        in_specs=[hbm] * 9,
        out_specs=(hbm, hbm, vmem),
        scratch_shapes=[
            *two(12, wy, HALF), *two(5, wy, HALF), *two(12, wx, HALF), *two(5, wx, HALF),
            *two(3, 1, HALF), *two(3, 1, HALF),
            pltpu.VMEM((ny, wx * wy, 2 * DIRS), f32),
            pltpu.VMEM((nx, 2, own, 2 * DIRS), f32),
            *[pltpu.VMEM((nx // 2, 2, own, 2 * DIRS), f32)] * 3,
            pltpu.VMEM((ny, 2 * rows, 3 * wx * wy), jnp.bfloat16),
            pltpu.SemaphoreType.DMA((6 * STEPS + 6,)), pltpu.SemaphoreType.DMA((6 * STEPS + 6,)),
            pltpu.SemaphoreType.DMA((ny,)), pltpu.SemaphoreType.DMA((ny,)),
            pltpu.SemaphoreType.DMA((nx,)), pltpu.SemaphoreType.DMA((nx,)),
            *[pltpu.VMEM(v.shape, v.dtype) for v in args[:6]],
            *[pltpu.SMEM(v.shape, v.dtype) for v in args[6:8]],
            pltpu.VMEM(args[8].shape, args[8].dtype),
            pltpu.SemaphoreType.DMA((13,)),
            pltpu.VMEM(te.shape, f32), pltpu.VMEM(th.shape, f32),
            pltpu.SemaphoreType.DMA((2,)),
        ],
        compiler_params=pltpu.CompilerParams(
            collective_id=0, has_side_effects=True, vmem_limit_bytes=64 * 1024 * 1024 - 65536
        ),
        name="slab",
    )(*args)
    return pl.pallas_call(
        hand_over,
        out_shape=out_shape,
        in_specs=[hbm] * 3,
        out_specs=(hbm, hbm, hbm),
        scratch_shapes=[pltpu.VMEM(v.shape, f32) for v in out_shape] + [pltpu.SemaphoreType.DMA((2, 7))],
        compiler_params=pltpu.CompilerParams(vmem_limit_bytes=64 * 1024 * 1024 - 65536),
        name="hand_over",
    )(*results)


def solution(mesh):
    in_specs = (
        P(None, "gx", "gy", None),
        P(None, "gx", "gy", None),
        P(None, "gx", "gy", None),
        P(None, "gx", "gy", None),
        P("gx", "gy", None),
        P("gx", "gy", None),
        P(),
        P(),
        P(),
    )
    out_specs = (P(None, "gx", "gy", None), P(None, "gx", "gy", None), P(("gx", "gy"), None))
    body = functools.partial(local, mesh.shape["gx"], mesh.shape["gy"])
    return jax.shard_map(body, mesh=mesh, in_specs=in_specs, out_specs=out_specs, check_vma=False)
```

```python
import functools
import math

import jax
import jax.numpy as jnp
from jax import lax
from jax.experimental import pallas as pl
from jax.experimental.pallas import tpu as pltpu
from jax.sharding import PartitionSpec as P

DIRS = 64
STEPS = 2
LAYERS = 4
WIDE = LAYERS * DIRS
HALF = WIDE // 2
time_step = 0.5


def lanes_of(shape):
    return lax.broadcasted_iota(jnp.int32, shape, len(shape) - 1)


def sublanes_of(shape):
    return lax.broadcasted_iota(jnp.int32, shape, len(shape) - 2)


def next_z(f):
    return jnp.where(lanes_of(f.shape) < WIDE - DIRS, pltpu.roll(f, WIDE - DIRS, f.ndim - 1), 0.0)


def prev_z(f):
    return jnp.where(lanes_of(f.shape) >= DIRS, pltpu.roll(f, DIRS, f.ndim - 1), 0.0)


def after_rows(f, row):
    n = f.shape[-2]
    return jnp.where(sublanes_of(f.shape) == n - 1, row, pltpu.roll(f, n - 1, f.ndim - 2))


def before_rows(f, row):
    return jnp.where(sublanes_of(f.shape) == 0, row, pltpu.roll(f, 1, f.ndim - 2))


def after_x(f, plane):
    return jnp.concatenate([f[1:], plane[None]], 0)


def before_x(f, plane):
    return jnp.concatenate([plane[None], f[:-1]], 0)


def packed(v):
    low, high = v[..., :HALF], v[..., HALF:]
    return jnp.where(lanes_of(low.shape) % DIRS < DIRS // 2, low, high)


def unpacked(v):
    near = lanes_of(v.shape) % DIRS < DIRS // 2
    axis = v.ndim - 1
    low = jnp.where(near, v, pltpu.roll(v, DIRS // 2, axis))
    high = jnp.where(near, pltpu.roll(v, HALF - DIRS // 2, axis), v)
    return jnp.concatenate([low, high], axis)


SHARE = 4
PIECE = DIRS // 2 // SHARE


def dense(planes):
    values = [packed(p) for p in planes]
    place = lanes_of(values[0].shape) % (DIRS // 2) // PIECE
    result = values[0]
    for q in range(1, len(values)):
        result = jnp.where(place == q, values[q], result)
    return result


def plane_of(v, q):
    place = lanes_of(v.shape) % (DIRS // 2) // PIECE
    result = v
    for r in range(SHARE):
        if r != q:
            result = jnp.where(place == r, pltpu.roll(v, (PIECE * (r - q)) % HALF, v.ndim - 1), result)
    return unpacked(result)


def take(buf, at, n):
    tangent = [jnp.concatenate([buf[at, 2 * k], buf[at, 2 * k + 1]], -1) for k in range(n)]
    forward = [plane_of(buf[at, 2 * n + k // SHARE], k % SHARE) for k in range(n)]
    return (tangent, forward)


def sine(turn):
    u = turn * (2.0 * math.pi)
    s = u * u
    poly = -1.0 / 39916800.0
    for c in (1.0 / 362880.0, -1.0 / 5040.0, 1.0 / 120.0, -1.0 / 6.0):
        poly = poly * s + c
    return u + u * (s * poly)


def half_step_h(e, h, rim):
    ex, ey, ez = e
    hx, hy, hz = h
    xp, yp, xm, ym, cx, cy = rim
    new = (
        hx - time_step * ((after_rows(ez, yp[1][:, None, :]) - ez) - (next_z(ey) - ey)),
        hy - time_step * ((next_z(ex) - ex) - (after_x(ez, xp[1]) - ez)),
        hz - time_step * ((after_x(ey, xp[0]) - ey) - (after_rows(ex, yp[0][:, None, :]) - ex)),
    )
    x_y = xm[3] - time_step * ((next_z(xm[0]) - xm[0]) - (ez[0] - xm[2]))
    x_z = xm[4] - time_step * ((ey[0] - xm[1]) - (after_rows(xm[0], cx) - xm[0]))
    y_x = ym[3] - time_step * ((ez[:, 0, :] - ym[2]) - (next_z(ym[1]) - ym[1]))
    y_z = ym[4] - time_step * ((after_rows(ym[1], cy) - ym[1]) - (ex[:, 0, :] - ym[0]))
    return new, (x_y, x_z, y_x, y_z)


def curl_b(h, rim):
    hx, hy, hz = h
    x_y, x_z, y_x, y_z = rim
    return (
        (hz - before_rows(hz, y_z[:, None, :])) - (hy - prev_z(hy)),
        (hx - prev_z(hx)) - (hz - before_x(hz, x_z)),
        (hy - before_x(hy, x_y)) - (hx - before_rows(hx, y_x[:, None, :])),
    )


def split(v):
    parts = []
    for _ in range(3):
        parts.append(v.astype(jnp.bfloat16))
        v = v - parts[-1].astype(jnp.float32)
    return parts


def widened(layers, ny):
    lead = layers[0].shape[0]
    flat = LAYERS * ny
    total = 0.0
    for z in range(LAYERS):
        for k, part in enumerate(split(layers[z])):
            place = (
                lax.broadcasted_iota(jnp.int32, (ny, 3 * flat), 1)
                == lax.broadcasted_iota(jnp.int32, (ny, 3 * flat), 0) + (k * flat + z * ny)
            ).astype(jnp.float32)
            total = total + jnp.dot(part, place.astype(jnp.bfloat16), preferred_element_type=jnp.float32)
    rows = jnp.broadcast_to(total[:, None, :], (lead, ny, 3 * flat))
    rows = jnp.where(lanes_of(rows.shape) % ny == sublanes_of(rows.shape), rows, 0.0)
    spread = (
        (lax.broadcasted_iota(jnp.int32, (3 * flat, WIDE), 0) // ny) % LAYERS
        == lax.broadcasted_iota(jnp.int32, (3 * flat, WIDE), 1) // DIRS
    ).astype(jnp.float32)
    wide = jnp.dot(
        rows.reshape(lead * ny, 3 * flat).astype(jnp.bfloat16),
        spread.astype(jnp.bfloat16),
        preferred_element_type=jnp.float32,
    )
    return wide.reshape(lead, ny, WIDE)


def kernel(
    nx, ny, own,
    te_at, th_at, fe_at, fh_at, classes_at, material_at, permittivity_at, contrast_at, orders_at,
    out_e, out_h, out_s,
    s_xm, r_xm, s_xp, r_xp, s_ym, r_ym, s_yp, r_yp, s_cx, r_cx, s_cy, r_cy,
    gathered, partial, paired, summed, arrived, table,
    rim_send, rim_recv, g_send, g_recv, p_send, p_recv,
    te, th, fe, fh, classes, material, permittivity, contrast, orders, load, new_e, new_h, store,
):
    loads = [
        pltpu.make_async_copy(src, dst, load.at[k])
        for k, (src, dst) in enumerate((
            *[(src.at[c], dst.at[c]) for c in range(3) for src, dst in ((te_at, te), (th_at, th))],
            (fe_at, fe), (fh_at, fh), (classes_at, classes),
            (material_at, material), (permittivity_at, permittivity), (contrast_at, contrast),
            (orders_at, orders),
        ))
    ]
    wx, wy = te.shape[1], te.shape[2]
    i, j = lax.axis_index("gx"), lax.axis_index("gy")
    up, down = lax.rem(i + 1, nx), lax.rem(i + nx - 1, nx)
    right, left = lax.rem(j + 1, ny), lax.rem(j + ny - 1, ny)
    barrier = pltpu.get_barrier_semaphore()
    offsets = sorted({1, nx - 1, *range(2, nx, 2)})
    peers = [(lax.rem(i + d, nx), j) for d in offsets]
    peers += [(i, lax.rem(j + d, ny)) for d in range(1, ny)]
    peers += [(up, left), (down, right)]
    for peer in peers:
        pl.semaphore_signal(barrier, inc=1, device_id=peer, device_id_type=pl.DeviceIdType.MESH)
    for c in loads:
        c.start()

    def copy(src, dst, send, recv, device):
        return pltpu.make_async_remote_copy(
            src_ref=src, dst_ref=dst, send_sem=send, recv_sem=recv,
            device_id=device, device_id_type=pl.DeviceIdType.MESH,
        )

    def planes_of(e, h):
        return (
            [f[:, wy - 1, :] for f in (e[0], e[1], e[2], h[0], h[2])],
            [f[wx - 1] for f in (e[0], e[1], e[2], h[1], h[2])],
            [e[0][:, 0, :], e[2][:, 0, :]],
            [e[1][0], e[2][0]],
            [e[0][wx - 1, 0:1, :]],
            [e[1][0, wy - 1:wy, :]],
        )

    rims = (
        (s_ym, r_ym, (i, right)), (s_xm, r_xm, (up, j)), (s_yp, r_yp, (i, left)),
        (s_xp, r_xp, (down, j)), (s_cx, r_cx, (up, left)), (s_cy, r_cy, (down, right)),
    )

    def put_tangent(step, e, h):
        for (buf, _, _), planes in zip(rims, planes_of(e, h)):
            for k, plane in enumerate(planes):
                buf[step, 2 * k] = plane[:, :HALF]
                buf[step, 2 * k + 1] = plane[:, HALF:]

    def put_forward(step, e, h):
        for (buf, _, _), planes in zip(rims, planes_of(e, h)):
            n = len(planes)
            for k in range(0, n, SHARE):
                buf[step, 2 * n + k // SHARE] = dense(planes[k:k + SHARE])

    def send(step, first, part):
        copies = []
        for k, (s, r, device) in enumerate(rims):
            n = (5, 5, 2, 2, 1, 1)[k]
            extra = s.shape[1] - 2 * n
            span = (pl.ds(0, 2 * n + extra), pl.ds(0, 2 * n), pl.ds(2 * n, extra))[part]
            copies.append(copy(
                s.at[step, span], r.at[step, span], rim_send.at[first + k], rim_recv.at[first + k], device
            ))
        for c in copies:
            c.start()
        return copies

    for c in loads[:6]:
        c.wait()
    e = [te[c] for c in range(3)]
    h = [th[c] for c in range(3)]
    put_tangent(0, e, h)
    pl.semaphore_wait(barrier, len(peers))
    waiting = send(0, 0, 1)
    for c in loads[6:]:
        c.wait()
    layers = []
    for z in range(LAYERS):
        layers.append(jnp.concatenate([
            fe[:, :, z, :].reshape(3 * wx, wy), fh[:, :, z, :].reshape(3 * wx, wy),
            classes[:, z, :].astype(jnp.float32), material[:, z, :].astype(jnp.float32),
        ], 0))
    wide = widened(layers, wy)
    fwd_e = [wide[c * wx:(c + 1) * wx] for c in range(3)]
    fwd_h = [wide[c * wx:(c + 1) * wx] for c in range(3, 6)]
    put_forward(0, fwd_e, fwd_h)
    waiting += send(0, 6, 2)

    kind = wide[7 * wx:]
    eps = jnp.zeros_like(kind)
    slope = jnp.zeros_like(kind)
    for k in range(permittivity.shape[0]):
        eps = jnp.where(kind == float(k), permittivity[k], eps)
        slope = jnp.where(kind == float(k), contrast[k], slope)
    inverse = time_step / eps
    coef = time_step * slope / (eps * eps)
    hot = wide[6 * wx:7 * wx] == (lanes_of(kind.shape) % DIRS).astype(jnp.float32)
    coef = jnp.where(hot, coef, 0.0)

    rows, cells = nx * own, ny * wx * wy
    count = orders.shape[1]
    row = lax.broadcasted_iota(jnp.int32, (rows, 1), 0)
    target = (row // own) * (ny * own) + j * own + row % own
    pick = (lax.broadcasted_iota(jnp.int32, (rows, count), 1) == target).astype(jnp.float32)
    pair = lax.dot_general(
        pick.astype(jnp.bfloat16), orders[...].astype(jnp.float32).astype(jnp.bfloat16),
        (((1,), (1,)), ((), ())), preferred_element_type=jnp.float32,
    )
    cell = lax.broadcasted_iota(jnp.int32, (1, cells), 1)
    all_x, all_y = nx * wx, ny * wy
    x_at = ((i * wx + (cell // wy) % wx) * all_y).astype(jnp.float32)
    y_at = (((cell // (wx * wy)) * wy + cell % wy) * all_x).astype(jnp.float32)
    index = pair[:, 0:1] * x_at + pair[:, 1:2] * y_at
    index = index - float(all_x * all_y) * jnp.round(index * (1.0 / (all_x * all_y)))
    turn = index * (1.0 / (all_x * all_y))
    cosine = sine(0.25 - jnp.abs(turn))
    sines = sine(jnp.where(turn > 0.25, 0.5 - turn, jnp.where(turn < -0.25, -0.5 - turn, turn)))
    block = wx * wy
    for at, value in ((0, cosine), (rows, sines)):
        near, far = split(value)[:2]
        for k in range(ny):
            for q, part in enumerate((near, far, near)):
                table[k, at:at + rows, q * block:(q + 1) * block] = part[:, k * block:(k + 1) * block]

    for step in range(STEPS):
        for c in waiting:
            c.wait()
        xm, ym = take(r_xm, step, 5), take(r_ym, step, 5)
        xp, yp = take(r_xp, step, 2), take(r_yp, step, 2)
        cx, cy = take(r_cx, step, 1), take(r_cy, step, 1)
        fwd_h, rim = half_step_h(fwd_e, fwd_h, (xp[1], yp[1], xm[1], ym[1], cx[1][0], cy[1][0]))
        fwd_c = curl_b(fwd_h, rim)
        fwd_e = [fwd_e[c] + inverse * fwd_c[c] for c in range(3)]
        h, rim = half_step_h(e, h, (xp[0], yp[0], xm[0], ym[0], cx[0][0], cy[0][0]))
        tan_c = curl_b(h, rim)
        e = [e[c] + inverse * tan_c[c] - coef * fwd_c[c] for c in range(3)]
        if step < STEPS - 1:
            put_tangent(step + 1, e, h)
            put_forward(step + 1, fwd_e, fwd_h)
            waiting = send(step + 1, 12 + 6 * step, 0)

    top_x, top_y = e[0][:, :, HALF:], e[1][:, :, HALF:]
    top = jnp.where(lanes_of(top_x.shape) < DIRS, pltpu.roll(top_x, DIRS, 2), top_y)
    gathered[j] = top.reshape(wx * wy, 2 * DIRS)
    copies = [
        copy(gathered.at[j], gathered.at[j], g_send.at[d], g_recv.at[d], (i, lax.rem(j + d, ny)))
        for d in range(1, ny)
    ]
    for c in copies:
        c.start()
    for c in range(3):
        new_e[c] = e[c]
        new_h[c] = h[c]
    stores = [
        pltpu.make_async_copy(new_e, out_e, store.at[0]),
        pltpu.make_async_copy(new_h, out_h, store.at[1]),
    ]
    for c in stores:
        c.start()
    def product(source):
        near, far = split(gathered[source])[:2]
        return jnp.dot(
            table[source], jnp.concatenate([near, near, far], 0), preferred_element_type=jnp.float32
        )

    sums = product(j)
    for d, c in zip(range(1, ny), copies):
        c.wait_recv()
        sums = sums + product(lax.rem(j + ny - d, ny))
    for c in copies:
        c.wait_send()
    for k in range(nx):
        partial[k, 0] = sums[k * own:(k + 1) * own]
        partial[k, 1] = sums[rows + k * own:rows + (k + 1) * own]
    core = lax.rem(i, 2)
    mate = i + 1 - 2 * core
    chips = nx // 2
    order = list(range(1, chips)) + [0]
    pairs = {
        d: copy(
            partial.at[lax.rem(mate + 2 * d, nx)], paired.at[d], p_send.at[d], p_recv.at[d], (mate, j)
        )
        for d in order
    }
    for d in order:
        pairs[d].start()
    copies = []
    for d in order:
        mine = lax.rem(i + 2 * d, nx)
        pairs[d].wait_recv()
        if d:
            summed[d] = partial[mine] + paired[d]
            c = copy(summed.at[d], arrived.at[d], p_send.at[chips + d], p_recv.at[chips + d], (mine, j))
            c.start()
            copies.append(c)
    total = partial[i] + paired[0]
    for d, c in zip(order, copies):
        c.wait_recv()
        total = total + arrived[d]
    for c in copies + [pairs[d] for d in order]:
        c.wait_send()
    scale = 1.0 / math.sqrt(all_x * all_y)
    re, im = total[0] * scale, total[1] * -scale
    low = lanes_of(re.shape) < DIRS
    out_s[:, :2 * DIRS] = jnp.where(low, re, pltpu.roll(im, DIRS, 1))
    out_s[:, 2 * DIRS:] = jnp.where(low, pltpu.roll(re, DIRS, 1), im)
    for c in stores:
        c.wait()


def hand_over(from_e, from_h, from_s, to_e, to_h, to_s, via_e, via_h, via_s, sem):
    plan = [
        (src.at[c], via.at[c], dst.at[c])
        for c in range(3) for src, via, dst in ((from_e, via_e, to_e), (from_h, via_h, to_h))
    ]
    plan.append((from_s, via_s, to_s))
    loads = [pltpu.make_async_copy(src, via, sem.at[0, k]) for k, (src, via, _) in enumerate(plan)]
    stores = [pltpu.make_async_copy(via, dst, sem.at[1, k]) for k, (_, via, dst) in enumerate(plan)]
    for c in loads:
        c.start()
    for load, store in zip(loads, stores):
        load.wait()
        store.start()
    for c in stores:
        c.wait()


def local(nx, ny, te, th, fe, fh, classes, material, permittivity, contrast, orders):
    wx, wy = te.shape[1], te.shape[2]
    own = orders.shape[0] // (nx * ny)
    rows = nx * own
    f32 = jnp.float32
    vmem = pl.BlockSpec(memory_space=pltpu.VMEM)
    args = (
        te, th, jnp.transpose(fe, (0, 1, 3, 2)), jnp.transpose(fh, (0, 1, 3, 2)),
        jnp.transpose(classes, (0, 2, 1)), jnp.transpose(material, (0, 2, 1)),
        permittivity, contrast, jnp.transpose(orders),
    )

    def two(*shape):
        return [pltpu.VMEM((STEPS,) + shape, f32)] * 2

    hbm = pl.BlockSpec(memory_space=pltpu.HBM)
    out_shape = (
        jax.ShapeDtypeStruct(te.shape, f32),
        jax.ShapeDtypeStruct(th.shape, f32),
        jax.ShapeDtypeStruct((own, 4 * DIRS), f32),
    )
    results = pl.pallas_call(
        functools.partial(kernel, nx, ny, own),
        out_shape=out_shape,
        in_specs=[hbm] * 9,
        out_specs=(hbm, hbm, vmem),
        scratch_shapes=[
            *two(12, wy, HALF), *two(5, wy, HALF), *two(12, wx, HALF), *two(5, wx, HALF),
            *two(3, 1, HALF), *two(3, 1, HALF),
            pltpu.VMEM((ny, wx * wy, 2 * DIRS), f32),
            pltpu.VMEM((nx, 2, own, 2 * DIRS), f32),
            *[pltpu.VMEM((nx // 2, 2, own, 2 * DIRS), f32)] * 3,
            pltpu.VMEM((ny, 2 * rows, 3 * wx * wy), jnp.bfloat16),
            pltpu.SemaphoreType.DMA((6 * STEPS + 6,)), pltpu.SemaphoreType.DMA((6 * STEPS + 6,)),
            pltpu.SemaphoreType.DMA((ny,)), pltpu.SemaphoreType.DMA((ny,)),
            pltpu.SemaphoreType.DMA((nx,)), pltpu.SemaphoreType.DMA((nx,)),
            *[pltpu.VMEM(v.shape, v.dtype) for v in args[:6]],
            *[pltpu.SMEM(v.shape, v.dtype) for v in args[6:8]],
            pltpu.VMEM(args[8].shape, args[8].dtype),
            pltpu.SemaphoreType.DMA((13,)),
            pltpu.VMEM(te.shape, f32), pltpu.VMEM(th.shape, f32),
            pltpu.SemaphoreType.DMA((2,)),
        ],
        compiler_params=pltpu.CompilerParams(
            collective_id=0, has_side_effects=True, vmem_limit_bytes=64 * 1024 * 1024 - 65536
        ),
        name="slab",
    )(*args)
    return pl.pallas_call(
        hand_over,
        out_shape=out_shape,
        in_specs=[hbm] * 3,
        out_specs=(hbm, hbm, hbm),
        scratch_shapes=[pltpu.VMEM(v.shape, f32) for v in out_shape] + [pltpu.SemaphoreType.DMA((2, 7))],
        compiler_params=pltpu.CompilerParams(vmem_limit_bytes=64 * 1024 * 1024 - 65536),
        name="hand_over",
    )(*results)


def solution(mesh):
    in_specs = (
        P(None, "gx", "gy", None),
        P(None, "gx", "gy", None),
        P(None, "gx", "gy", None),
        P(None, "gx", "gy", None),
        P("gx", "gy", None),
        P("gx", "gy", None),
        P(),
        P(),
        P(),
    )
    out_specs = (P(None, "gx", "gy", None), P(None, "gx", "gy", None), P(("gx", "gy"), None))
    body = functools.partial(local, mesh.shape["gx"], mesh.shape["gy"])
    return jax.shard_map(body, mesh=mesh, in_specs=in_specs, out_specs=out_specs, check_vma=False)
```
